32 devices in a mesh: outer: 2 (over x), inner: 4 (over y, core), cell: 4 (over z).
Axes of the slice: x: 2, y: 2, z: 4, core: 2. Of those that a mesh axis runs over, the one named last changes fastest.
Arguments:
- premium: float32 [48, 8192], P('outer', 'cell'), may hold values from 0.1 to 1
- charge: float32 [48, 8192], P('outer', 'cell'), may hold values from 0.05 to 2
- mortality: float32 [48, 8192], P('outer', 'cell'), may hold values from 0.0005 to 0.01
- lapse_table: float32 [16, 48], replicated, may hold values from 0.001 to 0.02
- lapse_index: int32 [8192], P('cell'), may hold values from 0 to 15
- guarantee_type: int32 [8192], P('cell'), may hold values from 0 to 2
- block_index: int32 [8192], P('cell'), may hold values from 0 to 255, never falling along the last dimension, each value on 1 to 128 neighbouring positions
- account_start: float32 [8192], P('cell'), may hold values from 5 to 50
- guarantee_start: float32 [8192], P('cell'), may hold values from 5 to 60
- fee_rate: float32 [8192], P('cell'), may hold values from 0.0003 to 0.002
- first_rates: float32 [8, 64, 36], P('outer', 'inner'), may hold values from 0 to 0.006
- second_rates: float32 [8, 64, 24], P('outer', 'inner'), may hold values from 0 to 0.006
- world_rates: float32 [8, 24], P('outer'), may hold values from 0 to 0.006
- spread: float32 [8], P('outer'), may hold values from 0.0005 to 0.002
Outputs:
- cell_reserve: float32 [2, 8, 8192], P(None, ('outer', 'inner'), 'cell')
- block_reserve: float32 [2, 8, 256], P(None, ('outer', 'inner'), 'cell')
- capital: float32 [1], replicated
The draws below stay inside these ranges and needn't reach their ends.
Inputs may be any that keep to these rules, and one draw needn't show every extreme that they name: `block_index`: block numbers never fall along the cells; every block holds 1 to 128 cells.
All inputs are finite; a program needn't handle non-finite values.
Results may differ from the reference program's by a relative error of at most 0.0003.
Values sent between devices are 32-bit elements; how exact they have to be, the bound alone decides.
A program may use at most 64 MiB of HBM per device.

```python
import math
import jax
import jax.numpy as jnp
import numpy as np
from jax import lax

PERIOD = 12
BLOCK = 128
LAPSE_TABLES = 16
MONTHS = 48
OUTER = 8
PATHS = 64
CELLS = 8192
NBLK = 256


def rate_paths(key, months):
    level_key, shock_key = jax.random.split(key, 2)
    level = jax.random.uniform(level_key, (OUTER, PATHS, 1), jnp.float32, 0.0, 0.006)
    shocks = 0.0004 * jax.random.normal(shock_key, (OUTER, PATHS, months), jnp.float32)
    walked = level + jnp.cumsum(shocks, axis=2)
    return jnp.clip(walked, 0.0, 0.006)


def draw_first_rates(key, part):
    return rate_paths(jax.random.fold_in(key, 11), MONTHS - PERIOD)


def draw_second_rates(key, part):
    return rate_paths(jax.random.fold_in(key, 12), MONTHS - 2 * PERIOD)


def draw_charge(key, part):
    group_key, value_key = jax.random.split(jax.random.fold_in(key, 21))
    heavy = jax.random.uniform(group_key, (1, CELLS), jnp.float32) < 0.125
    unit = jax.random.uniform(value_key, (MONTHS, CELLS), jnp.float32)
    light = 0.05 * jnp.exp(unit * math.log(10.0))
    dense = jnp.exp(unit * math.log(2.0))
    return jnp.where(heavy, dense, light)


def with_ends(values, rng, least, largest):
    index_at = [jax.random.randint(jax.random.fold_in(rng, axis), (), 0, length) for axis, length in enumerate(values.shape)]
    widest = values.shape.index(max(values.shape))
    beside = index_at[:widest] + [(index_at[widest] + 1) % values.shape[widest]] + index_at[widest + 1:]
    return values.at[tuple(index_at)].set(least).at[tuple(beside)].set(largest)


def block_levels(rng, shape, cuts, low, largest):
    gain, own = 1.0, jax.random.fold_in(rng, 6)
    for dim, blocks in cuts:
        heights = jnp.exp(jax.random.uniform(jax.random.fold_in(own, dim), (blocks,), jnp.float32, low / len(cuts), largest / len(cuts)))
        gain = gain * jnp.repeat(heights, shape[dim] // blocks).reshape([-1 if axis == dim else 1 for axis in range(len(shape))])
    return gain


def profile(number_of, total, limit, lean):
    weights = [(1 << 20) // math.isqrt(standing ** lean) + 1 for standing in range(2, number_of + 1)]
    spare, given = total - limit - (number_of - 1), [1] * (number_of - 1)
    while spare > 0:
        candidates = [i for i in range(number_of - 1) if given[i] < limit]
        mass, budget = sum([weights[i] for i in candidates]), spare
        for i in candidates:
            addition = min(limit - given[i], max(1, budget * weights[i] // mass), spare)
            given[i] = given[i] + addition
            spare = spare - addition
    return np.array([limit] + given)


def uneven_parts(stream_key, count, total, limit, skew):
    if count == 2:
        one = jax.random.randint(stream_key, (), max(1, total - limit), min(limit, total - 1) + 1)
        return jnp.stack([one, total - one])
    sizes = jnp.asarray(profile(count, total, limit, skew), jnp.int32)
    pairs = (count - 1) // 2
    donor, sink = sizes[1:1 + 2 * pairs:2], sizes[2:2 + 2 * pairs:2]
    slack = jnp.minimum(donor - 1, limit - sink)
    shifted = jax.random.randint(jax.random.fold_in(stream_key, 1), (pairs,), 0, 1 << 20) % (slack + 1)
    sizes = sizes.at[1:1 + 2 * pairs:2].set(donor - shifted).at[2:2 + 2 * pairs:2].set(sink + shifted)
    return sizes[jax.random.permutation(jax.random.fold_in(stream_key, 2), count)]


def setup_inputs(seed: int = 0) -> dict:
    key_of = jax.random.split(jax.random.key(seed), 15)
    return {
        "premium": jnp.clip(jnp.exp(math.log(1.0) - 2.3025851 * jax.random.uniform(key_of[0], (MONTHS, CELLS), jnp.float32) ** block_levels(key_of[0], (MONTHS, CELLS), ((0, 2), (1, 4)), -0.2, 0.2)), 0.1, 1.0),
        "charge": draw_charge(jax.random.fold_in(key_of[14], 71), 0),
        "mortality": jnp.clip(jnp.exp(math.log(0.01) - 2.9957322 * jax.random.uniform(key_of[2], (MONTHS, CELLS), jnp.float32) ** block_levels(key_of[2], (MONTHS, CELLS), ((0, 2), (1, 4)), -0.2, 0.2)), 0.0005, 0.01),
        "lapse_table": jnp.clip(jnp.exp(jax.random.uniform(key_of[3], (LAPSE_TABLES, MONTHS), jnp.float32, math.log(0.001), math.log(0.02))), 0.001, 0.02),
        "lapse_index": with_ends(jax.random.randint(key_of[4], (CELLS,), 0, LAPSE_TABLES), jax.random.fold_in(key_of[4], 1), 0, LAPSE_TABLES - 1).astype(jnp.int32),
        "guarantee_type": with_ends(jax.random.randint(key_of[5], (CELLS,), 0, 3), jax.random.fold_in(key_of[5], 1), 0, 2).astype(jnp.int32),
        "block_index": jnp.searchsorted(jnp.cumsum(uneven_parts(key_of[6], NBLK, CELLS, BLOCK, 1)), jnp.arange(CELLS), side="right").astype(jnp.int32),
        "account_start": jnp.clip(jnp.exp(math.log(50.0) - 2.3025851 * jax.random.uniform(key_of[7], (CELLS,), jnp.float32) ** block_levels(key_of[7], (CELLS,), ((0, 4),), -0.2, 0.2)), 5.0, 50.0),
        "guarantee_start": jnp.clip(jnp.exp(math.log(60.0) - 2.4849066 * jax.random.uniform(key_of[8], (CELLS,), jnp.float32) ** block_levels(key_of[8], (CELLS,), ((0, 4),), -0.2, 0.2)), 5.0, 60.0),
        "fee_rate": jnp.clip(jnp.exp(math.log(0.002) - 1.89712 * jax.random.uniform(key_of[9], (CELLS,), jnp.float32) ** block_levels(key_of[9], (CELLS,), ((0, 4),), -0.2, 0.2)), 0.0003, 0.002),
        "first_rates": draw_first_rates(jax.random.fold_in(key_of[14], 71), 0),
        "second_rates": draw_second_rates(jax.random.fold_in(key_of[14], 71), 0),
        "world_rates": jnp.clip(0.006 * jax.random.uniform(key_of[12], (OUTER, 2 * PERIOD), jnp.float32) ** block_levels(key_of[12], (OUTER, 2 * PERIOD), ((0, 2),), -0.2, 0.2), 0.0, 0.006),
        "spread": jnp.clip(0.0005 + 0.0015 * jax.random.uniform(key_of[13], (OUTER,), jnp.float32) ** block_levels(key_of[13], (OUTER,), ((0, 2),), -0.2, 0.2), 0.0005, 0.002),
    }


credit_floor = 0.001
rollup_growth = 0.05


def month_step(account, surviving, guarantee, log_discount, present, short_rate, net_flow, mortality, lapse_base, fee_rate, spread):
    rider_fee = fee_rate * account
    before = jnp.maximum(account + net_flow - rider_fee, 0.0)
    credited = before * (1.0 + jnp.maximum(short_rate - spread, credit_floor))
    log_discount = log_discount + short_rate
    lapse_rate = lapse_base * jnp.clip(credited / guarantee, 0.5, 1.5)
    claims = surviving * (mortality * jnp.maximum(guarantee - credited, 0.0) - rider_fee)
    present = present + jnp.exp(-log_discount) * claims
    surviving = surviving * (1.0 - mortality - lapse_rate)
    return credited, surviving, log_discount, present


def anniversary(account, guarantee, ratchet, rollup):
    return guarantee + ratchet * (jnp.maximum(guarantee, account) - guarantee) + rollup * rollup_growth * guarantee


def project_ref(account, surviving, guarantee, short_rates, start_month, spread, plans, fee_rate, ratchet, rollup):
    net_flow, mortality, lapse_base = plans
    log_discount = jnp.zeros((short_rates.shape[0], 1), jnp.float32)
    present = jnp.zeros((1, 1), jnp.float32)
    for offset in range(short_rates.shape[1]):
        calendar = start_month + offset
        account, surviving, log_discount, present = month_step(
            account, surviving, guarantee, log_discount, present, short_rates[:, offset:offset + 1],
            net_flow[calendar], mortality[calendar], lapse_base[calendar], fee_rate, spread)
        if (calendar + 1) % PERIOD == 0:
            guarantee = anniversary(account, guarantee, ratchet, rollup)
    return account, surviving, guarantee, present


def reference(premium, charge, mortality, lapse_table, lapse_index, guarantee_type, block_index, account_start, guarantee_start, fee_rate, first_rates, second_rates, world_rates, spread):
    net_flow = premium - charge
    lapse_base = lapse_table[lapse_index].T
    plans = (net_flow, mortality, lapse_base)
    ratchet = (guarantee_type == 1).astype(jnp.float32)
    rollup = (guarantee_type == 2).astype(jnp.float32)

    def one_outer(inputs):
        rates_one, rates_two, world_one, spread_one = inputs
        world_row = world_one[None, :]
        year_one = project_ref(account_start[None, :], jnp.ones((1, CELLS), jnp.float32), guarantee_start[None, :],
                               world_row[:, :PERIOD], 0, spread_one, plans, fee_rate, ratchet, rollup)
        inner_one = project_ref(year_one[0], year_one[1], year_one[2], rates_one, PERIOD, spread_one,
                                plans, fee_rate, ratchet, rollup)
        reserve_one = jnp.sum(inner_one[3], axis=0) / PATHS
        total_one = jnp.sum(reserve_one)
        spread_two = spread_one * (1.0 + jnp.tanh(total_one / CELLS))
        year_two = project_ref(year_one[0], year_one[1], year_one[2], world_row[:, PERIOD:], PERIOD, spread_two,
                               plans, fee_rate, ratchet, rollup)
        inner_two = project_ref(year_two[0], year_two[1], year_two[2], rates_two, 2 * PERIOD, spread_two,
                                plans, fee_rate, ratchet, rollup)
        reserve_two = jnp.sum(inner_two[3], axis=0) / PATHS
        total_two = jnp.sum(reserve_two)
        discount = jnp.exp(-jnp.sum(world_one[PERIOD:]))
        outer_loss = (discount * total_two - total_one) / CELLS
        return jnp.stack([reserve_one, reserve_two]), outer_loss

    reserves, losses = lax.map(one_outer, (first_rates, second_rates, world_rates, spread))
    cell_reserve = jnp.transpose(reserves, (1, 0, 2))
    block_hot = (block_index[:, None] == jnp.arange(NBLK)[None, :]).astype(jnp.float32)
    block_reserve = jnp.dot(cell_reserve.reshape(2 * OUTER, CELLS), block_hot,
                            precision=lax.Precision.HIGHEST).reshape(2, OUTER, NBLK)
    ordered = jnp.sort(losses)
    capital = jnp.mean(ordered[OUTER - OUTER // 4:]).reshape((1,))
    return cell_reserve, block_reserve, capital
```

```python
import functools
import jax
import jax.numpy as jnp
from jax import lax
from jax.experimental import pallas as pl
from jax.experimental.pallas import tpu as pltpu
from jax.sharding import PartitionSpec as P

PERIOD = 12
BLOCK = 128
LANES = 128
ROWS = 8

credit_floor = 0.001
rollup_growth = 0.05
VMEM = pl.BlockSpec(memory_space=pltpu.VMEM)


def tiles(x, count):
    return jnp.concatenate([x] * count, axis=1)


def month(account, surviving, growth, nf, om, lb, keep, inverse):
    credited = jnp.maximum(account * keep + nf, 0.0) * growth
    lapse = lb * jnp.clip(credited * inverse, 0.5, 1.5)
    return credited, surviving * (om - lapse)


def claims_of(account, credited, surviving, guarantee, mf):
    return surviving * (mf * jnp.maximum(guarantee - credited, 0.0) - account)


def anniversary(account, guarantee, ratchet, rollup):
    return (
        guarantee
        + ratchet * (jnp.maximum(guarantee, account) - guarantee)
        + rollup * rollup_growth * guarantee
    )


def prefix(rates):
    months = rates.shape[1]
    tri = (
        lax.broadcasted_iota(jnp.int32, (months, months), 0)
        <= lax.broadcasted_iota(jnp.int32, (months, months), 1)
    ).astype(jnp.float32)
    return jnp.dot(rates, tri, precision=lax.Precision.HIGHEST, preferred_element_type=jnp.float32)


def spread_lanes(values, target, rows):
    for m in range(values.shape[1]):
        target[m, rows, :] = jnp.broadcast_to(values[:, m : m + 1], (values.shape[0], LANES))


def year(start, plans, cell, growth_lanes, first_month, state, width):
    nf_ref, mf_ref, om_ref, lb_ref = plans
    total = nf_ref.shape[1]
    repeat = width // LANES

    def chunk(j, _):
        cols = pl.ds(pl.multiple_of(j * width, width), width)
        account, surviving, guarantee = start(cols)
        keep, ratchet, rollup = cell[0:1, cols], cell[1:2, cols], cell[2:3, cols]
        inverse = 1.0 / guarantee
        for m in range(PERIOD):
            row = slice(first_month + m, first_month + m + 1)
            account, surviving = month(
                account,
                surviving,
                tiles(growth_lanes[m], repeat),
                nf_ref[row, cols],
                om_ref[row, cols],
                lb_ref[row, cols],
                keep,
                inverse,
            )
        state[0, :, cols] = account
        state[1, :, cols] = surviving
        state[2, :, cols] = anniversary(account, guarantee, ratchet, rollup)
        return 0

    lax.fori_loop(0, total // width, chunk, 0)


def inner(state, plans, cell, gb, db, first_month, low, high, paths, sums, width):
    nf_ref, mf_ref, om_ref, lb_ref = plans
    total = nf_ref.shape[1]
    repeat = width // LANES
    months = db.shape[0]
    groups = paths // ROWS
    chunks = total // width

    def block(step, _):
        o, j = low + step // chunks, step % chunks
        cols = pl.ds(pl.multiple_of(j * width, width), width)
        keep, ratchet, rollup = cell[0:1, cols], cell[1:2, cols], cell[2:3, cols]
        shape = (ROWS, width)
        one = pl.ds(o, 1)
        account = [jnp.broadcast_to(state[0, one, cols], shape)] * groups
        surviving = [jnp.broadcast_to(state[1, one, cols], shape)] * groups
        guarantee = [jnp.broadcast_to(state[2, one, cols], shape)] * groups
        inverse = [1.0 / guarantee[0]] * groups
        rows = [pl.ds(pl.multiple_of(o * paths + g * ROWS, ROWS), ROWS) for g in range(groups)]
        present = jnp.zeros(shape, jnp.float32)
        for m in range(months):
            row = slice(first_month + m, first_month + m + 1)
            nf, mf, om, lb = nf_ref[row, cols], mf_ref[row, cols], om_ref[row, cols], lb_ref[row, cols]
            for g in range(groups):
                before, alive = account[g], surviving[g]
                account[g], surviving[g] = month(
                    before, alive, tiles(gb[m, rows[g], :], repeat), nf, om, lb, keep, inverse[g]
                )
                claims = claims_of(before, account[g], alive, guarantee[g], mf)
                present = present + tiles(db[m, rows[g], :], repeat) * claims
            if (m + 1) % PERIOD == 0 and m + 1 < months:
                for g in range(groups):
                    guarantee[g] = anniversary(account[g], guarantee[g], ratchet, rollup)
                    inverse[g] = 1.0 / guarantee[g]
        sums[o, :, cols] = present
        return 0

    lax.fori_loop(0, (high - low) * chunks, block, 0)


def reduce_rows(sums, out, low, high, scale):
    for o in range(low, high):
        out[o] = jnp.sum(sums[o], axis=0, keepdims=True) * scale


def fill_growth(rates_ref, spread_column, gb, low, high, paths):
    for o in range(low, high):
        for g in range(paths // ROWS):
            rows = slice(o * paths + g * ROWS, o * paths + (g + 1) * ROWS)
            spread_lanes(
                1.0 + jnp.maximum(rates_ref[rows, :] - spread_column[o : o + 1], credit_floor), gb, rows
            )


def fill_discount(rates_ref, db):
    discount = jnp.exp(-prefix(rates_ref[...]))
    for at in range(0, discount.shape[0], ROWS):
        spread_lanes(discount[at : at + ROWS], db, slice(at, at + ROWS))


def peers(axes):
    sizes = [lax.axis_size(axis) for axis in axes]
    count = 1
    place = 0
    for axis, size in zip(axes, sizes):
        place = place * size + lax.axis_index(axis)
        count *= size
    others = []
    for distance in range(1, count):
        index = lax.rem(place + distance, count)
        rest, device = index, {}
        for axis, size in reversed(list(zip(axes, sizes))):
            device[axis] = lax.rem(rest, size)
            rest = lax.div(rest, size)
        others.append((index, device))
    return place, others


def greet(groups):
    barrier = pltpu.get_barrier_semaphore()
    count = 0
    for others in groups:
        for _, device in others:
            pl.semaphore_signal(barrier, inc=1, device_id=device, device_id_type=pl.DeviceIdType.MESH)
            count += 1
    return barrier, count


def beside(me, size, act):
    @pl.when(me > 0)
    def _():
        act({"cell": me - 1})

    @pl.when(me < size - 1)
    def _():
        act({"cell": me + 1})

    return (me > 0).astype(jnp.int32) + (me < size - 1).astype(jnp.int32)


def signal_to(sem):
    def act(device):
        pl.semaphore_signal(sem, inc=1, device_id=device, device_id_type=pl.DeviceIdType.MESH)

    return act


def send(source, target, device, sems, at):
    copy = pltpu.make_async_remote_copy(
        src_ref=source,
        dst_ref=target,
        send_sem=sems.at[0, at],
        recv_sem=sems.at[1, at],
        device_id=device,
        device_id_type=pl.DeviceIdType.MESH,
    )
    copy.start()
    return copy


def finish(copies):
    for copy in copies:
        copy.wait()


def local_totals(partial, low, high):
    zero = jnp.zeros((1, LANES), jnp.float32)
    rows = [
        jnp.broadcast_to(jnp.sum(partial[o], axis=1, keepdims=True), (1, LANES)) if low <= o < high else zero
        for o in range(ROWS)
    ]
    return jnp.concatenate(rows, axis=0)


def whole_kernel(
    outers, paths, paths_all, cells_all, width,
    premium, charge, mortality, table_in, lapse_in, type_in, block_in, account_in, guarantee_in, fee_in,
    first_in, second_in, world_in, spread_in,
    reserve, block, capital,
    v_premium, v_charge, table, lapse, kind, block_row, account, guarantee, fee,
    first_rates, second_rates, world, spread,
    nf_all, mort_all, nf_ref, mf_ref, om_ref, lb_ref, cell, state_one, state_two,
    gb, db_one, db_two, gw, sums, first, second,
    slots_one, slots_two, kept_slots, hot, term_slots, term_out, loss_slots,
    load_sems, plan_sems, pass_sems, one_sems, total_sems, kept_sems, term_sems, loss_sems, relay_sems,
):
    outer_size, months_local, cells_local = nf_all.shape
    inner_size = kept_slots.shape[1]
    kept = reserve.shape[1]
    blocks = hot.shape[0]
    share = block.shape[3]
    group, group_others = peers(("inner", "cell"))
    inner_me, inner_others = peers(("inner",))
    cell_me, cell_others = peers(("cell",))
    outer_me, outer_others = peers(("outer",))
    barrier, arrivals = greet([inner_others, outer_others])
    cell_size = term_slots.shape[0]
    arrivals = arrivals + beside(cell_me, cell_size, signal_to(barrier))
    loads = [
        pltpu.make_async_copy(source, target, load_sems.at[i])
        for i, (source, target) in enumerate(
            [
                (premium, v_premium), (charge, v_charge), (mortality, mort_all.at[outer_me]),
                (table_in, table), (lapse_in, lapse), (type_in, kind), (block_in, block_row),
                (account_in, account), (guarantee_in, guarantee), (fee_in, fee),
                (first_in, first_rates), (second_in, second_rates), (world_in, world), (spread_in, spread),
            ]
        )
    ]
    for copy in loads:
        copy.start()
    finish(loads[:3])
    nf_all[outer_me] = v_premium[...] - v_charge[...]
    pl.semaphore_wait(barrier, arrivals)

    pair = inner_size % 2 == 0
    half = cells_local // 2 if pair else cells_local
    side = lax.rem(inner_me, 2) if pair else 0
    mine = pl.ds(pl.multiple_of(side * half, half), half)
    months_step = ROWS if months_local % ROWS == 0 else months_local
    plan_copies = []
    for at in range(0, months_local, months_step):
        part = []
        for d, (_, device) in enumerate(outer_others):
            for k, plan in enumerate((nf_all, mort_all)):
                rows = pl.ds(at, months_step)
                piece = plan.at[outer_me, rows, mine]
                slot = (at // months_step) * 2 * len(outer_others) + 2 * d + k
                part.append((d, plan, rows, slot, send(piece, piece, device, plan_sems, slot)))
        plan_copies.append(part)
    pass_copies = []

    def pass_on(part):
        for d, plan, rows, slot, copy in part:
            copy.wait_recv()
            if pair:
                source = lax.rem(outer_me + outer_size - 1 - d, outer_size)
                piece = plan.at[source, rows, mine]
                partner = {"inner": inner_me + 1 - 2 * side}
                pass_copies.append(send(piece, piece, partner, pass_sems, slot))

    rounds = relay_sems.shape[0]
    near = beside(cell_me, cell_size, signal_to(relay_sems.at[0]))
    finish(loads[3:])
    fee_row = fee[...]
    cell[0:1, :] = 1.0 - fee_row
    cell[1:2, :] = (kind[...] == 1).astype(jnp.float32)
    cell[2:3, :] = (kind[...] == 2).astype(jnp.float32)
    lapse_hot = (
        lax.broadcasted_iota(jnp.int32, (table.shape[0], cells_local), 0) == lapse[...]
    ).astype(jnp.float32)
    lb_ref[...] = lax.dot_general(
        table[...], lapse_hot, (((0,), (0,)), ((), ())),
        precision=lax.Precision.HIGHEST, preferred_element_type=jnp.float32,
    )
    world_rows = jnp.concatenate(
        [world[...], jnp.zeros((ROWS - outers, world.shape[1]), jnp.float32)], axis=0
    )
    diagonal = lax.broadcasted_iota(jnp.int32, (ROWS, outers), 0) == lax.broadcasted_iota(
        jnp.int32, (ROWS, outers), 1
    )
    spread_one = jnp.sum(jnp.where(diagonal, spread[...], 0.0), axis=1, keepdims=True)
    everything = slice(0, ROWS)
    spread_lanes(1.0 + jnp.maximum(world_rows[:, :PERIOD] - spread_one, credit_floor), gw, everything)
    fill_growth(first_rates, spread_one, gb, 0, outers, paths)
    parts = len(plan_copies)
    pass_on(plan_copies[0])
    fill_discount(first_rates, db_one)
    for part in plan_copies[1 : parts - 1]:
        pass_on(part)
    fill_discount(second_rates, db_two)
    if parts > 1:
        pass_on(plan_copies[parts - 1])
    hot[...] = (
        lax.broadcasted_iota(jnp.int32, (blocks, cells_local), 0) == block_row[...]
    ).astype(jnp.float32).astype(jnp.bfloat16)
    finish(pass_copies)
    death = 1.0 / fee_row
    for s in range(outer_size):
        rows = slice(s * months_local, (s + 1) * months_local)
        nf_ref[rows, :] = nf_all[s] * fee_row
        mf_ref[rows, :] = mort_all[s] * death
        om_ref[rows, :] = 1.0 - mort_all[s]
    plans = (nf_ref, mf_ref, om_ref, lb_ref)

    def start_one(cols):
        scale = fee[0:1, cols]
        shape = (ROWS, width)
        return (
            jnp.broadcast_to(account[0:1, cols] * scale, shape),
            jnp.ones(shape, jnp.float32),
            jnp.broadcast_to(guarantee[0:1, cols] * scale, shape),
        )

    def start_two(cols):
        return state_one[0, :, cols], state_one[1, :, cols], state_one[2, :, cols]

    for r in range(1, rounds):
        pl.semaphore_wait(relay_sems.at[r - 1], near)
        beside(cell_me, cell_size, signal_to(relay_sems.at[r]))
    year(start_one, plans, cell, gw, 0, state_one, width)
    split = -(-outers // 2)
    halves = [(low, high) for low, high in ((0, split), (split, outers)) if low < high]
    distances = len(group_others)
    one_copies = []
    for h, (low, high) in enumerate(halves):
        inner(state_one, plans, cell, gb, db_one, PERIOD, low, high, paths, sums, width)
        reduce_rows(sums, first, low, high, 1.0 / paths_all)
        slots_one[h, group] = local_totals(first, low, high)
        if h == 0:
            for part in plan_copies:
                for piece in part:
                    piece[4].wait_send()
            pl.semaphore_wait(relay_sems.at[rounds - 1], near)
        slot = slots_one.at[h, group]
        one_copies.append(
            [
                send(slot, slot, device, one_sems, h * distances + d)
                for d, (_, device) in enumerate(group_others)
            ]
        )
    kept_copies = []

    def send_kept(date, partial):
        for index, device in inner_others:
            kept_copies.append(
                send(
                    partial.at[pl.ds(index * kept, kept)], kept_slots.at[date, inner_me],
                    device, kept_sems, len(kept_copies),
                )
            )
        kept_slots[date, inner_me] = partial[pl.ds(inner_me * kept, kept)]

    send_kept(0, first)
    total_one = jnp.zeros((ROWS, LANES), jnp.float32)
    for h, (low, high) in enumerate(halves):
        finish(one_copies[h])
        total_one = total_one + jnp.sum(slots_one[h], axis=0)
        spread_two = (spread_one * (1.0 + jnp.tanh(total_one / cells_all)))[:, 0:1]
        spread_lanes(1.0 + jnp.maximum(world_rows[:, PERIOD:] - spread_two, credit_floor), gw, everything)
        year(start_two, plans, cell, gw, PERIOD, state_two, width)
        fill_growth(second_rates, spread_two, gb, low, high, paths)
        inner(state_two, plans, cell, gb, db_two, 2 * PERIOD, low, high, paths, sums, width)
        reduce_rows(sums, second, low, high, 1.0 / paths_all)
    slots_two[group] = local_totals(second, 0, outers)
    total_copies = [
        send(slots_two.at[group], slots_two.at[group], device, total_sems, d)
        for d, (_, device) in enumerate(group_others)
    ]
    send_kept(1, second)
    finish(kept_copies)
    held = [[jnp.sum(kept_slots[date, :, q], axis=0) for q in range(kept)] for date in range(2)]
    pieces = []
    for date in range(2):
        for q in range(kept):
            value = held[date][q]
            reserve[date, q] = value
            high = value.astype(jnp.bfloat16)
            value = value - high.astype(jnp.float32)
            middle = value.astype(jnp.bfloat16)
            low = (value - middle.astype(jnp.float32)).astype(jnp.bfloat16)
            pieces += [high.astype(jnp.float32), middle.astype(jnp.float32), low.astype(jnp.float32)]
    rows = term_slots.shape[1]
    missing = rows * 3 - len(pieces)
    stacked = jnp.concatenate(pieces + [jnp.zeros((missing, cells_local), jnp.float32)], axis=0)
    products = lax.dot_general(
        stacked.astype(jnp.bfloat16), hot[...], (((1,), (1,)), ((), ())),
        preferred_element_type=jnp.float32,
    )
    sums = [
        products[3 * i : 3 * i + 1] + products[3 * i + 1 : 3 * i + 2] + products[3 * i + 2 : 3 * i + 3]
        for i in range(rows)
    ]
    terms = jnp.concatenate(sums, axis=0)
    width = term_out.shape[2]
    for k in range(blocks // share):
        part = terms[:, k * share : (k + 1) * share]
        term_out[k] = jnp.concatenate([part, jnp.zeros((rows, width - share), jnp.float32)], axis=1)
    term_slots[cell_me] = term_out[cell_me]
    term_copies = [
        send(term_out.at[index], term_slots.at[cell_me], device, term_sems, d)
        for d, (index, device) in enumerate(cell_others)
    ]
    finish(total_copies)
    total_two = jnp.sum(slots_two[...], axis=0)
    discount = jnp.exp(-jnp.sum(world_rows[:, PERIOD:], axis=1, keepdims=True))
    loss_slots[outer_me] = (discount * total_two - total_one) / cells_all
    loss_copies = [
        send(loss_slots.at[outer_me], loss_slots.at[outer_me], device, loss_sems, d)
        for d, (_, device) in enumerate(outer_others)
    ]
    finish(term_copies)
    mine = jnp.sum(term_slots[...], axis=0)
    for date in range(2):
        for q in range(kept):
            i = date * kept + q
            block[date, q] = mine[i : i + 1, :share]
    finish(loss_copies)
    losses = jnp.concatenate([loss_slots[s, 0:outers] for s in range(loss_slots.shape[0])], axis=0)
    count = losses.shape[0]
    lane = lax.broadcasted_iota(jnp.int32, (count, LANES), 1)
    row = lax.broadcasted_iota(jnp.int32, (count, LANES), 0)
    across = jnp.sum(jnp.where(lane == row, losses, 0.0), axis=0, keepdims=True)
    ahead = ((across > losses) | ((across == losses) & (lane < row))) & (lane < count)
    rank = jnp.sum(jnp.where(ahead, 1.0, 0.0), axis=1, keepdims=True)
    top = count // 4
    taken = jnp.sum(jnp.where(rank < top, losses, 0.0), axis=0, keepdims=True) / top
    capital[...] = taken


def body(
    premium, charge, mortality, lapse_table, lapse_index, guarantee_type, block_index,
    account_start, guarantee_start, fee_rate, first_rates, second_rates, world_rates, spread,
):
    months_local, cells_local = premium.shape
    outer_size, inner_size, cell_size = (lax.axis_size(axis) for axis in ("outer", "inner", "cell"))
    months = months_local * outer_size
    group_size = inner_size * cell_size
    outers, paths = first_rates.shape[:2]
    paths_all = paths * inner_size
    cells_all = cells_local * cell_size
    width = 4 * LANES
    kept = outers // inner_size
    blocks = 4 * cells_all // BLOCK
    share = blocks // cell_size
    wide = -(-share // LANES) * LANES
    term_rows = -(-2 * kept // ROWS) * ROWS
    f32, i32 = jnp.float32, jnp.int32
    shape = jax.ShapeDtypeStruct

    def row(x):
        return x.reshape(1, -1)

    def buffer(*dims, dtype=f32):
        return pltpu.VMEM(dims, dtype)

    def sems(count):
        return pltpu.SemaphoreType.DMA((2, max(count, 1)))

    chunks = months_local // ROWS if months_local % ROWS == 0 else 1
    plan_count = 2 * chunks * (outer_size - 1)
    plan = buffer(months, cells_local)
    gathered = buffer(outer_size, months_local, cells_local)
    line, code = buffer(1, cells_local), buffer(1, cells_local, dtype=i32)
    total_rows = outers * paths
    first_months, second_months = first_rates.shape[2], second_rates.shape[2]
    operands = (
        premium, charge, mortality, lapse_table, row(lapse_index), row(guarantee_type), row(block_index),
        row(account_start), row(guarantee_start), row(fee_rate),
        first_rates.reshape(total_rows, -1), second_rates.reshape(total_rows, -1), world_rates, row(spread),
    )
    reserve, block, capital = pl.pallas_call(
        functools.partial(whole_kernel, outers, paths, paths_all, cells_all, width),
        out_shape=[
            shape((2, kept, 1, cells_local), f32), shape((2, kept, 1, share), f32), shape((1, LANES), f32),
        ],
        in_specs=[pl.BlockSpec(memory_space=pl.ANY)] * len(operands),
        out_specs=[VMEM] * 3,
        scratch_shapes=[
            buffer(months_local, cells_local), buffer(months_local, cells_local), buffer(*lapse_table.shape),
            code, code, code, line, line, line,
            buffer(total_rows, first_months), buffer(total_rows, second_months),
            buffer(*world_rates.shape), buffer(1, outers),
            gathered, gathered, plan, plan, plan, plan, buffer(ROWS, cells_local),
            buffer(3, ROWS, cells_local), buffer(3, ROWS, cells_local),
            buffer(first_months, total_rows, LANES), buffer(first_months, total_rows, LANES),
            buffer(second_months, total_rows, LANES), buffer(PERIOD, ROWS, LANES),
            buffer(outers, ROWS, cells_local), buffer(outers, 1, cells_local), buffer(outers, 1, cells_local),
            buffer(2, group_size, ROWS, LANES), buffer(group_size, ROWS, LANES),
            buffer(2, inner_size, kept, 1, cells_local), buffer(blocks, cells_local, dtype=jnp.bfloat16),
            buffer(cell_size, term_rows, wide), buffer(cell_size, term_rows, wide),
            buffer(outer_size, ROWS, LANES),
            pltpu.SemaphoreType.DMA((len(operands),)), sems(plan_count), sems(plan_count),
            sems(2 * (group_size - 1)), sems(group_size - 1), sems(2 * (inner_size - 1)),
            sems(cell_size - 1), sems(outer_size - 1), pltpu.SemaphoreType.REGULAR((max(cell_size - 1, 1),)),
        ],
        compiler_params=pltpu.CompilerParams(
            collective_id=0, has_side_effects=True, vmem_limit_bytes=60 * 2**20
        ),
    )(*operands)
    return (
        reserve.reshape(2, kept, cells_local),
        block.reshape(2, kept, share),
        capital[0, :1],
    )


def solution(mesh):
    placed = (
        P("outer", "cell"), P("outer", "cell"), P("outer", "cell"), P(), P("cell"), P("cell"), P("cell"),
        P("cell"), P("cell"), P("cell"), P("outer", "inner", None), P("outer", "inner", None),
        P("outer", None), P("outer"),
    )
    return jax.shard_map(
        body,
        mesh=mesh,
        in_specs=placed,
        out_specs=(P(None, ("outer", "inner"), "cell"), P(None, ("outer", "inner"), "cell"), P()),
        check_vma=False,
    )
```

```python
import functools
import jax
import jax.numpy as jnp
from jax import lax
from jax.experimental import pallas as pl
from jax.experimental.pallas import tpu as pltpu
from jax.sharding import PartitionSpec as P

PERIOD = 12
BLOCK = 128
LANES = 128
ROWS = 8
DIRECT = 32

credit_floor = 0.001
rollup_growth = 0.05
VMEM = pl.BlockSpec(memory_space=pltpu.VMEM)


def tiles(x, count):
    return jnp.concatenate([x] * count, axis=1)


def month(account, surviving, growth, nf, om, lb, keep, inverse):
    credited = jnp.maximum(account * keep + nf, 0.0) * growth
    lapse = lb * jnp.clip(credited * inverse, 0.5, 1.5)
    return credited, surviving * (om - lapse)


def claims_of(account, credited, surviving, guarantee, mf):
    return surviving * (mf * jnp.maximum(guarantee - credited, 0.0) - account)


def anniversary(account, guarantee, ratchet, rollup):
    return (
        guarantee
        + ratchet * (jnp.maximum(guarantee, account) - guarantee)
        + rollup * rollup_growth * guarantee
    )


def prefix(rates):
    months = rates.shape[1]
    tri = (
        lax.broadcasted_iota(jnp.int32, (months, months), 0)
        <= lax.broadcasted_iota(jnp.int32, (months, months), 1)
    ).astype(jnp.float32)
    return jnp.dot(rates, tri, precision=lax.Precision.HIGHEST, preferred_element_type=jnp.float32)


def spread_lanes(values, target, rows):
    for m in range(values.shape[1]):
        target[m, rows, :] = jnp.broadcast_to(values[:, m : m + 1], (values.shape[0], LANES))


def year(start, plans, cell, growth_lanes, first_month, state, width):
    nf_ref, mf_ref, om_ref, lb_ref = plans
    total = nf_ref.shape[1]
    repeat = width // LANES

    def chunk(j, _):
        cols = pl.ds(pl.multiple_of(j * width, width), width)
        account, surviving, guarantee = start(cols)
        keep, ratchet, rollup = cell[0:1, cols], cell[1:2, cols], cell[2:3, cols]
        inverse = 1.0 / guarantee
        for m in range(PERIOD):
            row = slice(first_month + m, first_month + m + 1)
            account, surviving = month(
                account,
                surviving,
                tiles(growth_lanes[m], repeat),
                nf_ref[row, cols],
                om_ref[row, cols],
                lb_ref[row, cols],
                keep,
                inverse,
            )
        state[0, :, cols] = account
        state[1, :, cols] = surviving
        state[2, :, cols] = anniversary(account, guarantee, ratchet, rollup)
        return 0

    lax.fori_loop(0, total // width, chunk, 0)


def inner(state, plans, cell, gb, db, first_month, low, high, paths, sums, width):
    nf_ref, mf_ref, om_ref, lb_ref = plans
    total = nf_ref.shape[1]
    repeat = width // LANES
    months = db.shape[0]
    groups = paths // ROWS
    chunks = total // width

    def block(step, _):
        o, j = low + step // chunks, step % chunks
        cols = pl.ds(pl.multiple_of(j * width, width), width)
        keep, ratchet, rollup = cell[0:1, cols], cell[1:2, cols], cell[2:3, cols]
        shape = (ROWS, width)
        one = pl.ds(o, 1)
        account = [jnp.broadcast_to(state[0, one, cols], shape)] * groups
        surviving = [jnp.broadcast_to(state[1, one, cols], shape)] * groups
        guarantee = [jnp.broadcast_to(state[2, one, cols], shape)] * groups
        inverse = [1.0 / guarantee[0]] * groups
        rows = [pl.ds(pl.multiple_of(o * paths + g * ROWS, ROWS), ROWS) for g in range(groups)]
        present = jnp.zeros(shape, jnp.float32)
        for m in range(months):
            row = slice(first_month + m, first_month + m + 1)
            nf, mf, om, lb = nf_ref[row, cols], mf_ref[row, cols], om_ref[row, cols], lb_ref[row, cols]
            for g in range(groups):
                before, alive = account[g], surviving[g]
                account[g], surviving[g] = month(
                    before, alive, tiles(gb[m, rows[g], :], repeat), nf, om, lb, keep, inverse[g]
                )
                claims = claims_of(before, account[g], alive, guarantee[g], mf)
                present = present + tiles(db[m, rows[g], :], repeat) * claims
            if (m + 1) % PERIOD == 0 and m + 1 < months:
                for g in range(groups):
                    guarantee[g] = anniversary(account[g], guarantee[g], ratchet, rollup)
                    inverse[g] = 1.0 / guarantee[g]
        sums[o, :, cols] = present
        return 0

    lax.fori_loop(0, (high - low) * chunks, block, 0)


def reduce_rows(sums, out, low, high, scale):
    for o in range(low, high):
        out[o] = jnp.sum(sums[o], axis=0, keepdims=True) * scale


def fill_growth(rates_ref, spread_column, gb, low, high, paths):
    for o in range(low, high):
        for g in range(paths // ROWS):
            rows = slice(o * paths + g * ROWS, o * paths + (g + 1) * ROWS)
            spread_lanes(
                1.0 + jnp.maximum(rates_ref[rows, :] - spread_column[o : o + 1], credit_floor), gb, rows
            )


def fill_discount(rates_ref, db):
    discount = jnp.exp(-prefix(rates_ref[...]))
    for at in range(0, discount.shape[0], ROWS):
        spread_lanes(discount[at : at + ROWS], db, slice(at, at + ROWS))


def peers(axes):
    sizes = [lax.axis_size(axis) for axis in axes]
    count = 1
    place = 0
    for axis, size in zip(axes, sizes):
        place = place * size + lax.axis_index(axis)
        count *= size
    others = []
    for distance in range(1, count):
        index = lax.rem(place + distance, count)
        rest, device = index, {}
        for axis, size in reversed(list(zip(axes, sizes))):
            device[axis] = lax.rem(rest, size)
            rest = lax.div(rest, size)
        others.append((index, device))
    return place, others


def greet(groups):
    barrier = pltpu.get_barrier_semaphore()
    count = 0
    for others in groups:
        for _, device in others:
            pl.semaphore_signal(barrier, inc=1, device_id=device, device_id_type=pl.DeviceIdType.MESH)
            count += 1
    return barrier, count


def beside(me, size, act):
    @pl.when(me > 0)
    def _():
        act({"cell": me - 1})

    @pl.when(me < size - 1)
    def _():
        act({"cell": me + 1})

    return (me > 0).astype(jnp.int32) + (me < size - 1).astype(jnp.int32)


def signal_to(sem):
    def act(device):
        pl.semaphore_signal(sem, inc=1, device_id=device, device_id_type=pl.DeviceIdType.MESH)

    return act


def send(source, target, device, sems, at):
    copy = pltpu.make_async_remote_copy(
        src_ref=source,
        dst_ref=target,
        send_sem=sems.at[0, at],
        recv_sem=sems.at[1, at],
        device_id=device,
        device_id_type=pl.DeviceIdType.MESH,
    )
    copy.start()
    return copy


def finish(copies):
    for copy in copies:
        copy.wait()


def local_totals(partial, low, high):
    zero = jnp.zeros((1, LANES), jnp.float32)
    rows = [
        jnp.broadcast_to(jnp.sum(partial[o], axis=1, keepdims=True), (1, LANES)) if low <= o < high else zero
        for o in range(ROWS)
    ]
    return jnp.concatenate(rows, axis=0)


def whole_kernel(
    outers, paths, paths_all, cells_all, width,
    premium, charge, mortality, table_in, lapse_in, type_in, block_in, account_in, guarantee_in, fee_in,
    first_in, second_in, world_in, spread_in,
    reserve, block, capital,
    v_premium, v_charge, table, lapse, kind, block_row, account, guarantee, fee,
    first_rates, second_rates, world, spread,
    nf_all, mort_all, nf_ref, mf_ref, om_ref, lb_ref, cell, state_one, state_two,
    gb, db_one, db_two, gw, sums, first, second,
    slots_one, slots_two, kept_slots, hot, term_slots, term_out, loss_slots,
    load_sems, plan_sems, pass_sems, one_sems, total_sems, kept_sems, term_sems, loss_sems, relay_sems,
):
    outer_size, months_local, cells_local = nf_all.shape
    inner_size = kept_slots.shape[1]
    cell_size = term_out.shape[0]
    kept = reserve.shape[1]
    blocks = hot.shape[0]
    share = block.shape[3]
    group, group_others = peers(("inner", "cell"))
    inner_me, inner_others = peers(("inner",))
    cell_me, cell_others = peers(("cell",))
    outer_me, outer_others = peers(("outer",))
    direct = slots_two.shape[0] > inner_size * cell_size
    all_me, all_others = peers(("outer", "inner", "cell")) if direct else (group, group_others)
    barrier, arrivals = greet([inner_others, outer_others])
    arrivals = arrivals + beside(cell_me, cell_size, signal_to(barrier))
    loads = [
        pltpu.make_async_copy(source, target, load_sems.at[i])
        for i, (source, target) in enumerate(
            [
                (premium, v_premium), (charge, v_charge), (mortality, mort_all.at[outer_me]),
                (table_in, table), (lapse_in, lapse), (type_in, kind), (block_in, block_row),
                (account_in, account), (guarantee_in, guarantee), (fee_in, fee),
                (first_in, first_rates), (second_in, second_rates), (world_in, world), (spread_in, spread),
            ]
        )
    ]
    for copy in loads:
        copy.start()
    finish(loads[:3])
    nf_all[outer_me] = v_premium[...] - v_charge[...]
    pl.semaphore_wait(barrier, arrivals)

    pair = inner_size % 2 == 0
    half = cells_local // 2 if pair else cells_local
    side = lax.rem(inner_me, 2) if pair else 0
    mine = pl.ds(pl.multiple_of(side * half, half), half)
    months_step = ROWS if months_local % ROWS == 0 else months_local
    plan_copies = []
    for at in range(0, months_local, months_step):
        part = []
        for d, (_, device) in enumerate(outer_others):
            for k, plan in enumerate((nf_all, mort_all)):
                rows = pl.ds(at, months_step)
                piece = plan.at[outer_me, rows, mine]
                slot = (at // months_step) * 2 * len(outer_others) + 2 * d + k
                part.append((d, plan, rows, slot, send(piece, piece, device, plan_sems, slot)))
        plan_copies.append(part)
    pass_copies = []

    def pass_on(part):
        for d, plan, rows, slot, copy in part:
            copy.wait_recv()
            if pair:
                source = lax.rem(outer_me + outer_size - 1 - d, outer_size)
                piece = plan.at[source, rows, mine]
                partner = {"inner": inner_me + 1 - 2 * side}
                pass_copies.append(send(piece, piece, partner, pass_sems, slot))

    rounds = relay_sems.shape[0]
    near = beside(cell_me, cell_size, signal_to(relay_sems.at[0]))
    finish(loads[3:])
    fee_row = fee[...]
    cell[0:1, :] = 1.0 - fee_row
    cell[1:2, :] = (kind[...] == 1).astype(jnp.float32)
    cell[2:3, :] = (kind[...] == 2).astype(jnp.float32)
    lapse_hot = (
        lax.broadcasted_iota(jnp.int32, (table.shape[0], cells_local), 0) == lapse[...]
    ).astype(jnp.float32)
    lb_ref[...] = lax.dot_general(
        table[...], lapse_hot, (((0,), (0,)), ((), ())),
        precision=lax.Precision.HIGHEST, preferred_element_type=jnp.float32,
    )
    world_rows = jnp.concatenate(
        [world[...], jnp.zeros((ROWS - outers, world.shape[1]), jnp.float32)], axis=0
    )
    diagonal = lax.broadcasted_iota(jnp.int32, (ROWS, outers), 0) == lax.broadcasted_iota(
        jnp.int32, (ROWS, outers), 1
    )
    spread_one = jnp.sum(jnp.where(diagonal, spread[...], 0.0), axis=1, keepdims=True)
    everything = slice(0, ROWS)
    spread_lanes(1.0 + jnp.maximum(world_rows[:, :PERIOD] - spread_one, credit_floor), gw, everything)
    fill_growth(first_rates, spread_one, gb, 0, outers, paths)
    parts = len(plan_copies)
    pass_on(plan_copies[0])
    fill_discount(first_rates, db_one)
    for part in plan_copies[1 : parts - 1]:
        pass_on(part)
    fill_discount(second_rates, db_two)
    if parts > 1:
        pass_on(plan_copies[parts - 1])
    hot[...] = (
        lax.broadcasted_iota(jnp.int32, (blocks, cells_local), 0) == block_row[...]
    ).astype(jnp.float32).astype(jnp.bfloat16)
    finish(pass_copies)
    death = 1.0 / fee_row
    for s in range(outer_size):
        rows = slice(s * months_local, (s + 1) * months_local)
        nf_ref[rows, :] = nf_all[s] * fee_row
        mf_ref[rows, :] = mort_all[s] * death
        om_ref[rows, :] = 1.0 - mort_all[s]
    plans = (nf_ref, mf_ref, om_ref, lb_ref)

    def start_one(cols):
        scale = fee[0:1, cols]
        shape = (ROWS, width)
        return (
            jnp.broadcast_to(account[0:1, cols] * scale, shape),
            jnp.ones(shape, jnp.float32),
            jnp.broadcast_to(guarantee[0:1, cols] * scale, shape),
        )

    def start_two(cols):
        return state_one[0, :, cols], state_one[1, :, cols], state_one[2, :, cols]

    for r in range(1, rounds):
        pl.semaphore_wait(relay_sems.at[r - 1], near)
        beside(cell_me, cell_size, signal_to(relay_sems.at[r]))
    year(start_one, plans, cell, gw, 0, state_one, width)
    split = -(-outers // 2)
    halves = [(low, high) for low, high in ((0, split), (split, outers)) if low < high]
    distances = len(group_others)
    one_copies = []
    for h, (low, high) in enumerate(halves):
        inner(state_one, plans, cell, gb, db_one, PERIOD, low, high, paths, sums, width)
        reduce_rows(sums, first, low, high, 1.0 / paths_all)
        slots_one[h, group] = local_totals(first, low, high)
        if h == 0:
            for part in plan_copies:
                for piece in part:
                    piece[4].wait_send()
            pl.semaphore_wait(relay_sems.at[rounds - 1], near)
        slot = slots_one.at[h, group]
        one_copies.append(
            [
                send(slot, slot, device, one_sems, h * distances + d)
                for d, (_, device) in enumerate(group_others)
            ]
        )
    kept_copies = []

    def send_kept(date, partial):
        for index, device in inner_others:
            kept_copies.append(
                send(
                    partial.at[pl.ds(index * kept, kept)], kept_slots.at[date, inner_me],
                    device, kept_sems, len(kept_copies),
                )
            )
        kept_slots[date, inner_me] = partial[pl.ds(inner_me * kept, kept)]

    send_kept(0, first)
    total_one = jnp.zeros((ROWS, LANES), jnp.float32)
    for h, (low, high) in enumerate(halves):
        finish(one_copies[h])
        total_one = total_one + jnp.sum(slots_one[h], axis=0)
        spread_two = (spread_one * (1.0 + jnp.tanh(total_one / cells_all)))[:, 0:1]
        spread_lanes(1.0 + jnp.maximum(world_rows[:, PERIOD:] - spread_two, credit_floor), gw, everything)
        year(start_two, plans, cell, gw, PERIOD, state_two, width)
        fill_growth(second_rates, spread_two, gb, low, high, paths)
        inner(state_two, plans, cell, gb, db_two, 2 * PERIOD, low, high, paths, sums, width)
        reduce_rows(sums, second, low, high, 1.0 / paths_all)
    discount = jnp.exp(-jnp.sum(world_rows[:, PERIOD:], axis=1, keepdims=True))
    mine_one = slots_one[0, group]
    for h in range(1, len(halves)):
        mine_one = mine_one + slots_one[h, group]
    mine_loss = (discount * local_totals(second, 0, outers) - mine_one) / cells_all
    own = lax.broadcasted_iota(jnp.int32, (ROWS, LANES), 0)
    own_lane = lax.broadcasted_iota(jnp.int32, (ROWS, LANES), 1) - outer_me * outers
    mine_loss = jnp.where((own == own_lane) & (own < outers), mine_loss, 0.0)
    place, others = (all_me, all_others) if direct else (group, group_others)
    slots_two[place] = jnp.sum(mine_loss, axis=0, keepdims=True)
    total_copies = [
        send(slots_two.at[place], slots_two.at[place], device, total_sems, d)
        for d, (_, device) in enumerate(others)
    ]
    send_kept(1, second)
    step = -(-outers // ROWS) * ROWS
    lines = 2 * step
    line = lax.broadcasted_iota(jnp.int32, (step, cells_local), 0)
    values = []
    for partial in (first, second):
        value = jnp.zeros((step, cells_local), jnp.float32)
        for o in range(outers):
            value = jnp.where(line == o, jnp.broadcast_to(partial[o], value.shape), value)
        values.append(value)
    value = jnp.concatenate(values, axis=0)
    high = value.astype(jnp.bfloat16).astype(jnp.float32)
    value = value - high
    middle = value.astype(jnp.bfloat16).astype(jnp.float32)
    stacked = jnp.concatenate([high, middle, value - middle], axis=0)
    products = lax.dot_general(
        stacked.astype(jnp.bfloat16), hot[...], (((1,), (1,)), ((), ())),
        preferred_element_type=jnp.float32,
    )
    terms = products[:lines] + products[lines : 2 * lines] + products[2 * lines :]
    width = term_out.shape[3]
    for k in range(cell_size):
        spot = slice(k * share, (k + 1) * share)
        part = [terms[:step, spot], terms[step:, spot]]
        if width > 2 * share:
            part.append(jnp.zeros((step, width - 2 * share), jnp.float32))
        part = jnp.concatenate(part, axis=1)
        for o in range(outers):
            term_out[k, o] = part[o : o + 1]
    term_slots[group] = term_out[cell_me, pl.ds(inner_me * kept, kept)]
    term_copies = [
        send(
            term_out.at[lax.rem(index, cell_size), pl.ds(lax.div(index, cell_size) * kept, kept)],
            term_slots.at[group], device, term_sems, d,
        )
        for d, (index, device) in enumerate(group_others)
    ]
    finish(kept_copies)
    for date in range(2):
        for q in range(kept):
            reserve[date, q] = jnp.sum(kept_slots[date, :, q], axis=0)
    finish(term_copies)
    for q in range(kept):
        mine = jnp.sum(term_slots[:, q], axis=0)
        for date in range(2):
            block[date, q] = mine[:, date * share : (date + 1) * share]
    finish(total_copies)
    across = jnp.sum(slots_two[...], axis=0)
    if not direct:
        loss_slots[outer_me] = across
        finish(
            [
                send(loss_slots.at[outer_me], loss_slots.at[outer_me], device, loss_sems, d)
                for d, (_, device) in enumerate(outer_others)
            ]
        )
        across = jnp.sum(loss_slots[...], axis=0)
    count = outers * outer_size
    lane = lax.broadcasted_iota(jnp.int32, (count, LANES), 1)
    row = lax.broadcasted_iota(jnp.int32, (count, LANES), 0)
    losses = jnp.sum(jnp.where(lane == row, across, 0.0), axis=1, keepdims=True)
    ahead = ((across > losses) | ((across == losses) & (lane < row))) & (lane < count)
    rank = jnp.sum(jnp.where(ahead, 1.0, 0.0), axis=1, keepdims=True)
    top = count // 4
    taken = jnp.sum(jnp.where(rank < top, losses, 0.0), axis=0, keepdims=True) / top
    capital[...] = jnp.broadcast_to(taken, capital.shape)


def body(
    premium, charge, mortality, lapse_table, lapse_index, guarantee_type, block_index,
    account_start, guarantee_start, fee_rate, first_rates, second_rates, world_rates, spread,
):
    months_local, cells_local = premium.shape
    outer_size, inner_size, cell_size = (lax.axis_size(axis) for axis in ("outer", "inner", "cell"))
    months = months_local * outer_size
    group_size = inner_size * cell_size
    outers, paths = first_rates.shape[:2]
    paths_all = paths * inner_size
    cells_all = cells_local * cell_size
    width = 4 * LANES
    kept = outers // inner_size
    blocks = 4 * cells_all // BLOCK
    share = blocks // cell_size
    wide = -(-2 * share // LANES) * LANES
    everyone = outer_size * group_size
    wide_count = everyone if everyone <= DIRECT else group_size
    f32, i32 = jnp.float32, jnp.int32
    shape = jax.ShapeDtypeStruct

    def row(x):
        return x.reshape(1, -1)

    def buffer(*dims, dtype=f32):
        return pltpu.VMEM(dims, dtype)

    def sems(count):
        return pltpu.SemaphoreType.DMA((2, max(count, 1)))

    chunks = months_local // ROWS if months_local % ROWS == 0 else 1
    plan_count = 2 * chunks * (outer_size - 1)
    plan = buffer(months, cells_local)
    gathered = buffer(outer_size, months_local, cells_local)
    line, code = buffer(1, cells_local), buffer(1, cells_local, dtype=i32)
    total_rows = outers * paths
    first_months, second_months = first_rates.shape[2], second_rates.shape[2]
    operands = (
        premium, charge, mortality, lapse_table, row(lapse_index), row(guarantee_type), row(block_index),
        row(account_start), row(guarantee_start), row(fee_rate),
        first_rates.reshape(total_rows, -1), second_rates.reshape(total_rows, -1), world_rates, row(spread),
    )
    reserve, block, capital = pl.pallas_call(
        functools.partial(whole_kernel, outers, paths, paths_all, cells_all, width),
        out_shape=[
            shape((2, kept, 1, cells_local), f32), shape((2, kept, 1, share), f32), shape((1, LANES), f32),
        ],
        in_specs=[pl.BlockSpec(memory_space=pl.ANY)] * len(operands),
        out_specs=[VMEM] * 3,
        scratch_shapes=[
            buffer(months_local, cells_local), buffer(months_local, cells_local), buffer(*lapse_table.shape),
            code, code, code, line, line, line,
            buffer(total_rows, first_months), buffer(total_rows, second_months),
            buffer(*world_rates.shape), buffer(1, outers),
            gathered, gathered, plan, plan, plan, plan, buffer(ROWS, cells_local),
            buffer(3, ROWS, cells_local), buffer(3, ROWS, cells_local),
            buffer(first_months, total_rows, LANES), buffer(first_months, total_rows, LANES),
            buffer(second_months, total_rows, LANES), buffer(PERIOD, ROWS, LANES),
            buffer(outers, ROWS, cells_local), buffer(outers, 1, cells_local), buffer(outers, 1, cells_local),
            buffer(2, group_size, ROWS, LANES), buffer(wide_count, 1, LANES),
            buffer(2, inner_size, kept, 1, cells_local), buffer(blocks, cells_local, dtype=jnp.bfloat16),
            buffer(group_size, kept, 1, wide), buffer(cell_size, outers, 1, wide),
            buffer(outer_size, 1, LANES),
            pltpu.SemaphoreType.DMA((len(operands),)), sems(plan_count), sems(plan_count),
            sems(2 * (group_size - 1)), sems(wide_count - 1), sems(2 * (inner_size - 1)),
            sems(group_size - 1), sems(outer_size - 1), pltpu.SemaphoreType.REGULAR((max(cell_size - 1, 1),)),
        ],
        compiler_params=pltpu.CompilerParams(
            collective_id=0, has_side_effects=True, vmem_limit_bytes=24*2**20
        ),
    )(*[pltpu.with_memory_space_constraint(x, pltpu.HBM) for x in operands])
    return (
        reserve.reshape(2, kept, cells_local),
        block.reshape(2, kept, share),
        capital[0, :1],
    )


def solution(mesh):
    placed = (
        P("outer", "cell"), P("outer", "cell"), P("outer", "cell"), P(), P("cell"), P("cell"), P("cell"),
        P("cell"), P("cell"), P("cell"), P("outer", "inner", None), P("outer", "inner", None),
        P("outer", None), P("outer"),
    )
    return jax.shard_map(
        body,
        mesh=mesh,
        in_specs=placed,
        out_specs=(P(None, ("outer", "inner"), "cell"), P(None, ("outer", "inner"), "cell"), P()),
        check_vma=False,
    )
```

```python
import functools
import jax
import jax.numpy as jnp
from jax import lax
from jax.experimental import pallas as pl
from jax.experimental.pallas import tpu as pltpu
from jax.sharding import PartitionSpec as P

PERIOD = 12
BLOCK = 128
LANES = 128
ROWS = 8
DIRECT = 32

credit_floor = 0.001
rollup_growth = 0.05
VMEM = pl.BlockSpec(memory_space=pltpu.VMEM)


def tiles(x, count):
    return jnp.concatenate([x] * count, axis=1)


def month(account, surviving, growth, nf, om, lb, keep, inverse):
    credited = jnp.maximum(account * keep + nf, 0.0) * growth
    lapse = lb * jnp.clip(credited * inverse, 0.5, 1.5)
    return credited, surviving * (om - lapse)


def claims_of(account, credited, surviving, guarantee, mf):
    return surviving * (mf * jnp.maximum(guarantee - credited, 0.0) - account)


def anniversary(account, guarantee, ratchet, rollup):
    return (
        guarantee
        + ratchet * (jnp.maximum(guarantee, account) - guarantee)
        + rollup * rollup_growth * guarantee
    )


def prefix(rates):
    months = rates.shape[1]
    tri = (
        lax.broadcasted_iota(jnp.int32, (months, months), 0)
        <= lax.broadcasted_iota(jnp.int32, (months, months), 1)
    ).astype(jnp.float32)
    return jnp.dot(rates, tri, precision=lax.Precision.HIGHEST, preferred_element_type=jnp.float32)


def spread_lanes(values, target, rows):
    for m in range(values.shape[1]):
        target[m, rows, :] = jnp.broadcast_to(values[:, m : m + 1], (values.shape[0], LANES))


def year(start, plans, cell, growth_lanes, first_month, state, width):
    nf_ref, mf_ref, om_ref, lb_ref = plans
    total = nf_ref.shape[1]
    repeat = width // LANES

    def chunk(j, _):
        cols = pl.ds(pl.multiple_of(j * width, width), width)
        account, surviving, guarantee = start(cols)
        keep, ratchet, rollup = cell[0:1, cols], cell[1:2, cols], cell[2:3, cols]
        inverse = 1.0 / guarantee
        for m in range(PERIOD):
            row = slice(first_month + m, first_month + m + 1)
            account, surviving = month(
                account,
                surviving,
                tiles(growth_lanes[m], repeat),
                nf_ref[row, cols],
                om_ref[row, cols],
                lb_ref[row, cols],
                keep,
                inverse,
            )
        state[0, :, cols] = account
        state[1, :, cols] = surviving
        state[2, :, cols] = anniversary(account, guarantee, ratchet, rollup)
        return 0

    lax.fori_loop(0, total // width, chunk, 0)


def inner(state, plans, cell, gb, db, first_month, low, high, paths, sums, width):
    nf_ref, mf_ref, om_ref, lb_ref = plans
    total = nf_ref.shape[1]
    repeat = width // LANES
    months = db.shape[0]
    groups = paths // ROWS
    chunks = total // width

    def block(step, _):
        o, j = low + step // chunks, step % chunks
        cols = pl.ds(pl.multiple_of(j * width, width), width)
        keep, ratchet, rollup = cell[0:1, cols], cell[1:2, cols], cell[2:3, cols]
        shape = (ROWS, width)
        one = pl.ds(o, 1)
        account = [jnp.broadcast_to(state[0, one, cols], shape)] * groups
        surviving = [jnp.broadcast_to(state[1, one, cols], shape)] * groups
        guarantee = [jnp.broadcast_to(state[2, one, cols], shape)] * groups
        inverse = [1.0 / guarantee[0]] * groups
        rows = [pl.ds(pl.multiple_of(o * paths + g * ROWS, ROWS), ROWS) for g in range(groups)]
        present = jnp.zeros(shape, jnp.float32)
        for m in range(months):
            row = slice(first_month + m, first_month + m + 1)
            nf, mf, om, lb = nf_ref[row, cols], mf_ref[row, cols], om_ref[row, cols], lb_ref[row, cols]
            for g in range(groups):
                before, alive = account[g], surviving[g]
                account[g], surviving[g] = month(
                    before, alive, tiles(gb[m, rows[g], :], repeat), nf, om, lb, keep, inverse[g]
                )
                claims = claims_of(before, account[g], alive, guarantee[g], mf)
                present = present + tiles(db[m, rows[g], :], repeat) * claims
            if (m + 1) % PERIOD == 0 and m + 1 < months:
                for g in range(groups):
                    guarantee[g] = anniversary(account[g], guarantee[g], ratchet, rollup)
                    inverse[g] = 1.0 / guarantee[g]
        sums[o, :, cols] = present
        return 0

    lax.fori_loop(0, (high - low) * chunks, block, 0)


def reduce_rows(sums, out, low, high, scale):
    for o in range(low, high):
        out[o] = jnp.sum(sums[o], axis=0, keepdims=True) * scale


def fill_growth(rates_ref, spread_column, gb, low, high, paths):
    for o in range(low, high):
        for g in range(paths // ROWS):
            rows = slice(o * paths + g * ROWS, o * paths + (g + 1) * ROWS)
            spread_lanes(
                1.0 + jnp.maximum(rates_ref[rows, :] - spread_column[o : o + 1], credit_floor), gb, rows
            )


def fill_discount(rates_ref, db):
    discount = jnp.exp(-prefix(rates_ref[...]))
    for at in range(0, discount.shape[0], ROWS):
        spread_lanes(discount[at : at + ROWS], db, slice(at, at + ROWS))


def peers(axes):
    sizes = [lax.axis_size(axis) for axis in axes]
    count = 1
    place = 0
    for axis, size in zip(axes, sizes):
        place = place * size + lax.axis_index(axis)
        count *= size
    others = []
    for distance in range(1, count):
        index = lax.rem(place + distance, count)
        rest, device = index, {}
        for axis, size in reversed(list(zip(axes, sizes))):
            device[axis] = lax.rem(rest, size)
            rest = lax.div(rest, size)
        others.append((index, device))
    return place, others


def greet(groups):
    barrier = pltpu.get_barrier_semaphore()
    count = 0
    for others in groups:
        for _, device in others:
            pl.semaphore_signal(barrier, inc=1, device_id=device, device_id_type=pl.DeviceIdType.MESH)
            count += 1
    return barrier, count


def beside(me, size, act):
    @pl.when(me > 0)
    def _():
        act({"cell": me - 1})

    @pl.when(me < size - 1)
    def _():
        act({"cell": me + 1})

    return (me > 0).astype(jnp.int32) + (me < size - 1).astype(jnp.int32)


def signal_to(sem):
    def act(device):
        pl.semaphore_signal(sem, inc=1, device_id=device, device_id_type=pl.DeviceIdType.MESH)

    return act


def send(source, target, device, sems, at):
    copy = pltpu.make_async_remote_copy(
        src_ref=source,
        dst_ref=target,
        send_sem=sems.at[0, at],
        recv_sem=sems.at[1, at],
        device_id=device,
        device_id_type=pl.DeviceIdType.MESH,
    )
    copy.start()
    return copy


def finish(copies):
    for copy in copies:
        copy.wait()


def local_totals(partial, low, high):
    zero = jnp.zeros((1, LANES), jnp.float32)
    rows = [
        jnp.broadcast_to(jnp.sum(partial[o], axis=1, keepdims=True), (1, LANES)) if low <= o < high else zero
        for o in range(ROWS)
    ]
    return jnp.concatenate(rows, axis=0)


def whole_kernel(
    outers, paths, paths_all, cells_all, width,
    premium, charge, mortality, table_in, lapse_in, type_in, block_in, account_in, guarantee_in, fee_in,
    first_in, second_in, world_in, spread_in,
    reserve, block, capital,
    v_premium, v_charge, table, lapse, kind, block_row, account, guarantee, fee,
    first_rates, second_rates, world, spread,
    nf_all, mort_all, nf_ref, mf_ref, om_ref, lb_ref, cell, state_one, state_two,
    gb, db_one, db_two, gw, sums, first, second,
    slots_one, slots_two, kept_slots, hot, term_slots, term_out, loss_slots,
    load_sems, plan_sems, pass_sems, one_sems, total_sems, kept_sems, term_sems, loss_sems, relay_sems,
):
    outer_size, months_local, cells_local = nf_all.shape
    inner_size = kept_slots.shape[1]
    cell_size = term_out.shape[0]
    kept = reserve.shape[1]
    blocks = hot.shape[0]
    share = block.shape[3]
    group, group_others = peers(("inner", "cell"))
    inner_me, inner_others = peers(("inner",))
    cell_me, cell_others = peers(("cell",))
    outer_me, outer_others = peers(("outer",))
    direct = slots_two.shape[0] > inner_size * cell_size
    all_me, all_others = peers(("outer", "inner", "cell")) if direct else (group, group_others)
    barrier, arrivals = greet([inner_others, outer_others])
    arrivals = arrivals + beside(cell_me, cell_size, signal_to(barrier))
    loads = [
        pltpu.make_async_copy(source, target, load_sems.at[i])
        for i, (source, target) in enumerate(
            [
                (premium, v_premium), (charge, v_charge), (mortality, mort_all.at[outer_me]),
                (table_in, table), (lapse_in, lapse), (type_in, kind), (block_in, block_row),
                (account_in, account), (guarantee_in, guarantee), (fee_in, fee),
                (first_in, first_rates), (second_in, second_rates), (world_in, world), (spread_in, spread),
            ]
        )
    ]
    for copy in loads:
        copy.start()
    finish(loads[:3])
    nf_all[outer_me] = v_premium[...] - v_charge[...]
    pl.semaphore_wait(barrier, arrivals)

    pair = inner_size % 2 == 0
    half = cells_local // 2 if pair else cells_local
    side = lax.rem(inner_me, 2) if pair else 0
    mine = pl.ds(pl.multiple_of(side * half, half), half)
    months_step = ROWS if months_local % ROWS == 0 else months_local
    plan_copies = []
    for at in range(0, months_local, months_step):
        part = []
        for d, (_, device) in enumerate(outer_others):
            for k, plan in enumerate((nf_all, mort_all)):
                rows = pl.ds(at, months_step)
                piece = plan.at[outer_me, rows, mine]
                slot = (at // months_step) * 2 * len(outer_others) + 2 * d + k
                part.append((d, plan, rows, slot, send(piece, piece, device, plan_sems, slot)))
        plan_copies.append(part)
    pass_copies = []

    def pass_on(part):
        for d, plan, rows, slot, copy in part:
            copy.wait_recv()
            if pair:
                source = lax.rem(outer_me + outer_size - 1 - d, outer_size)
                piece = plan.at[source, rows, mine]
                partner = {"inner": inner_me + 1 - 2 * side}
                pass_copies.append(send(piece, piece, partner, pass_sems, slot))

    rounds = relay_sems.shape[0]

    def relay(low, high):
        for r in range(low, min(high, rounds)):
            pl.semaphore_wait(relay_sems.at[r - 1], near)
            beside(cell_me, cell_size, signal_to(relay_sems.at[r]))

    near = beside(cell_me, cell_size, signal_to(relay_sems.at[0]))
    finish(loads[3:])
    fee_row = fee[...]
    cell[0:1, :] = 1.0 - fee_row
    cell[1:2, :] = (kind[...] == 1).astype(jnp.float32)
    cell[2:3, :] = (kind[...] == 2).astype(jnp.float32)
    lapse_hot = (
        lax.broadcasted_iota(jnp.int32, (table.shape[0], cells_local), 0) == lapse[...]
    ).astype(jnp.float32)
    lb_ref[...] = lax.dot_general(
        table[...], lapse_hot, (((0,), (0,)), ((), ())),
        precision=lax.Precision.HIGHEST, preferred_element_type=jnp.float32,
    )
    world_rows = jnp.concatenate(
        [world[...], jnp.zeros((ROWS - outers, world.shape[1]), jnp.float32)], axis=0
    )
    diagonal = lax.broadcasted_iota(jnp.int32, (ROWS, outers), 0) == lax.broadcasted_iota(
        jnp.int32, (ROWS, outers), 1
    )
    spread_one = jnp.sum(jnp.where(diagonal, spread[...], 0.0), axis=1, keepdims=True)
    everything = slice(0, ROWS)
    spread_lanes(1.0 + jnp.maximum(world_rows[:, :PERIOD] - spread_one, credit_floor), gw, everything)
    fill_growth(first_rates, spread_one, gb, 0, outers, paths)
    parts = len(plan_copies)
    pass_on(plan_copies[0])
    relay(1, 2)
    fill_discount(first_rates, db_one)
    for part in plan_copies[1 : parts - 1]:
        pass_on(part)
    fill_discount(second_rates, db_two)
    if parts > 1:
        pass_on(plan_copies[parts - 1])
    hot[...] = (
        lax.broadcasted_iota(jnp.int32, (blocks, cells_local), 0) == block_row[...]
    ).astype(jnp.float32).astype(jnp.bfloat16)
    relay(2, rounds)
    finish(pass_copies)
    death = 1.0 / fee_row
    for s in range(outer_size):
        rows = slice(s * months_local, (s + 1) * months_local)
        nf_ref[rows, :] = nf_all[s] * fee_row
        mf_ref[rows, :] = mort_all[s] * death
        om_ref[rows, :] = 1.0 - mort_all[s]
    plans = (nf_ref, mf_ref, om_ref, lb_ref)

    def start_one(cols):
        scale = fee[0:1, cols]
        shape = (ROWS, width)
        return (
            jnp.broadcast_to(account[0:1, cols] * scale, shape),
            jnp.ones(shape, jnp.float32),
            jnp.broadcast_to(guarantee[0:1, cols] * scale, shape),
        )

    def start_two(cols):
        return state_one[0, :, cols], state_one[1, :, cols], state_one[2, :, cols]

    year(start_one, plans, cell, gw, 0, state_one, width)
    split = -(-outers // 2)
    halves = [(low, high) for low, high in ((0, split), (split, outers)) if low < high]
    distances = len(group_others)
    one_copies = []
    for h, (low, high) in enumerate(halves):
        inner(state_one, plans, cell, gb, db_one, PERIOD, low, high, paths, sums, width)
        reduce_rows(sums, first, low, high, 1.0 / paths_all)
        slots_one[h, group] = local_totals(first, low, high)
        if h == 0:
            for part in plan_copies:
                for piece in part:
                    piece[4].wait_send()
            pl.semaphore_wait(relay_sems.at[rounds - 1], near)
        slot = slots_one.at[h, group]
        one_copies.append(
            [
                send(slot, slot, device, one_sems, h * distances + d)
                for d, (_, device) in enumerate(group_others)
            ]
        )
    kept_copies = []

    def send_kept(date, partial):
        for index, device in inner_others:
            kept_copies.append(
                send(
                    partial.at[pl.ds(index * kept, kept)], kept_slots.at[date, inner_me],
                    device, kept_sems, len(kept_copies),
                )
            )
        kept_slots[date, inner_me] = partial[pl.ds(inner_me * kept, kept)]

    send_kept(0, first)
    total_one = jnp.zeros((ROWS, LANES), jnp.float32)
    for h, (low, high) in enumerate(halves):
        finish(one_copies[h])
        total_one = total_one + jnp.sum(slots_one[h], axis=0)
        spread_two = (spread_one * (1.0 + jnp.tanh(total_one / cells_all)))[:, 0:1]
        spread_lanes(1.0 + jnp.maximum(world_rows[:, PERIOD:] - spread_two, credit_floor), gw, everything)
        year(start_two, plans, cell, gw, PERIOD, state_two, width)
        fill_growth(second_rates, spread_two, gb, low, high, paths)
        inner(state_two, plans, cell, gb, db_two, 2 * PERIOD, low, high, paths, sums, width)
        reduce_rows(sums, second, low, high, 1.0 / paths_all)
    discount = jnp.exp(-jnp.sum(world_rows[:, PERIOD:], axis=1, keepdims=True))
    mine_one = slots_one[0, group]
    for h in range(1, len(halves)):
        mine_one = mine_one + slots_one[h, group]
    mine_loss = (discount * local_totals(second, 0, outers) - mine_one) / cells_all
    own = lax.broadcasted_iota(jnp.int32, (ROWS, LANES), 0)
    own_lane = lax.broadcasted_iota(jnp.int32, (ROWS, LANES), 1) - outer_me * outers
    mine_loss = jnp.where((own == own_lane) & (own < outers), mine_loss, 0.0)
    place, others = (all_me, all_others) if direct else (group, group_others)
    slots_two[place] = jnp.sum(mine_loss, axis=0, keepdims=True)
    total_copies = [
        send(slots_two.at[place], slots_two.at[place], device, total_sems, d)
        for d, (_, device) in enumerate(others)
    ]
    send_kept(1, second)
    step = -(-outers // ROWS) * ROWS
    lines = 2 * step
    line = lax.broadcasted_iota(jnp.int32, (step, cells_local), 0)
    values = []
    for partial in (first, second):
        value = jnp.zeros((step, cells_local), jnp.float32)
        for o in range(outers):
            value = jnp.where(line == o, jnp.broadcast_to(partial[o], value.shape), value)
        values.append(value)
    value = jnp.concatenate(values, axis=0)
    high = value.astype(jnp.bfloat16).astype(jnp.float32)
    value = value - high
    middle = value.astype(jnp.bfloat16).astype(jnp.float32)
    stacked = jnp.concatenate([high, middle, value - middle], axis=0)
    products = lax.dot_general(
        stacked.astype(jnp.bfloat16), hot[...], (((1,), (1,)), ((), ())),
        preferred_element_type=jnp.float32,
    )
    terms = products[:lines] + products[lines : 2 * lines] + products[2 * lines :]
    width = term_out.shape[3]
    for k in range(cell_size):
        spot = slice(k * share, (k + 1) * share)
        part = [terms[:step, spot], terms[step:, spot]]
        if width > 2 * share:
            part.append(jnp.zeros((step, width - 2 * share), jnp.float32))
        part = jnp.concatenate(part, axis=1)
        for o in range(outers):
            term_out[k, o] = part[o : o + 1]
    term_slots[group] = term_out[cell_me, pl.ds(inner_me * kept, kept)]
    term_copies = [
        send(
            term_out.at[lax.rem(index, cell_size), pl.ds(lax.div(index, cell_size) * kept, kept)],
            term_slots.at[group], device, term_sems, d,
        )
        for d, (index, device) in enumerate(group_others)
    ]
    finish(kept_copies)
    for date in range(2):
        for q in range(kept):
            reserve[date, q] = jnp.sum(kept_slots[date, :, q], axis=0)
    finish(term_copies)
    for q in range(kept):
        mine = jnp.sum(term_slots[:, q], axis=0)
        for date in range(2):
            block[date, q] = mine[:, date * share : (date + 1) * share]
    finish(total_copies)
    across = jnp.sum(slots_two[...], axis=0)
    if not direct:
        loss_slots[outer_me] = across
        finish(
            [
                send(loss_slots.at[outer_me], loss_slots.at[outer_me], device, loss_sems, d)
                for d, (_, device) in enumerate(outer_others)
            ]
        )
        across = jnp.sum(loss_slots[...], axis=0)
    count = outers * outer_size
    lane = lax.broadcasted_iota(jnp.int32, (count, LANES), 1)
    row = lax.broadcasted_iota(jnp.int32, (count, LANES), 0)
    losses = jnp.sum(jnp.where(lane == row, across, 0.0), axis=1, keepdims=True)
    ahead = ((across > losses) | ((across == losses) & (lane < row))) & (lane < count)
    rank = jnp.sum(jnp.where(ahead, 1.0, 0.0), axis=1, keepdims=True)
    top = count // 4
    taken = jnp.sum(jnp.where(rank < top, losses, 0.0), axis=0, keepdims=True) / top
    capital[...] = jnp.broadcast_to(taken, capital.shape)


def settle(reserve, block, capital, reserve_out, block_out, capital_out, single, sems):
    single[...] = capital[:, :1]
    copies = [
        pltpu.make_async_copy(source, target, sems.at[i])
        for i, (source, target) in enumerate(
            [(reserve, reserve_out), (block, block_out), (single, capital_out)]
        )
    ]
    for copy in copies:
        copy.start()
    finish(copies)


def body(
    premium, charge, mortality, lapse_table, lapse_index, guarantee_type, block_index,
    account_start, guarantee_start, fee_rate, first_rates, second_rates, world_rates, spread,
):
    months_local, cells_local = premium.shape
    outer_size, inner_size, cell_size = (lax.axis_size(axis) for axis in ("outer", "inner", "cell"))
    months = months_local * outer_size
    group_size = inner_size * cell_size
    outers, paths = first_rates.shape[:2]
    paths_all = paths * inner_size
    cells_all = cells_local * cell_size
    width = 4 * LANES
    kept = outers // inner_size
    blocks = 4 * cells_all // BLOCK
    share = blocks // cell_size
    wide = -(-2 * share // LANES) * LANES
    everyone = outer_size * group_size
    wide_count = everyone if everyone <= DIRECT else group_size
    f32, i32 = jnp.float32, jnp.int32
    shape = jax.ShapeDtypeStruct

    def row(x):
        return x.reshape(1, -1)

    def buffer(*dims, dtype=f32):
        return pltpu.VMEM(dims, dtype)

    def sems(count):
        return pltpu.SemaphoreType.DMA((2, max(count, 1)))

    chunks = months_local // ROWS if months_local % ROWS == 0 else 1
    plan_count = 2 * chunks * (outer_size - 1)
    plan = buffer(months, cells_local)
    gathered = buffer(outer_size, months_local, cells_local)
    line, code = buffer(1, cells_local), buffer(1, cells_local, dtype=i32)
    total_rows = outers * paths
    first_months, second_months = first_rates.shape[2], second_rates.shape[2]
    operands = (
        premium, charge, mortality, lapse_table, row(lapse_index), row(guarantee_type), row(block_index),
        row(account_start), row(guarantee_start), row(fee_rate),
        first_rates.reshape(total_rows, -1), second_rates.reshape(total_rows, -1), world_rates, row(spread),
    )
    reserve, block, capital = pl.pallas_call(
        functools.partial(whole_kernel, outers, paths, paths_all, cells_all, width),
        out_shape=[
            shape((2, kept, 1, cells_local), f32), shape((2, kept, 1, share), f32), shape((1, LANES), f32),
        ],
        in_specs=[pl.BlockSpec(memory_space=pl.ANY)] * len(operands),
        out_specs=[VMEM] * 3,
        scratch_shapes=[
            buffer(months_local, cells_local), buffer(months_local, cells_local), buffer(*lapse_table.shape),
            code, code, code, line, line, line,
            buffer(total_rows, first_months), buffer(total_rows, second_months),
            buffer(*world_rates.shape), buffer(1, outers),
            gathered, gathered, plan, plan, plan, plan, buffer(ROWS, cells_local),
            buffer(3, ROWS, cells_local), buffer(3, ROWS, cells_local),
            buffer(first_months, total_rows, LANES), buffer(first_months, total_rows, LANES),
            buffer(second_months, total_rows, LANES), buffer(PERIOD, ROWS, LANES),
            buffer(outers, ROWS, cells_local), buffer(outers, 1, cells_local), buffer(outers, 1, cells_local),
            buffer(2, group_size, ROWS, LANES), buffer(wide_count, 1, LANES),
            buffer(2, inner_size, kept, 1, cells_local), buffer(blocks, cells_local, dtype=jnp.bfloat16),
            buffer(group_size, kept, 1, wide), buffer(cell_size, outers, 1, wide),
            buffer(outer_size, 1, LANES),
            pltpu.SemaphoreType.DMA((len(operands),)), sems(plan_count), sems(plan_count),
            sems(2 * (group_size - 1)), sems(wide_count - 1), sems(2 * (inner_size - 1)),
            sems(group_size - 1), sems(outer_size - 1), pltpu.SemaphoreType.REGULAR((max(cell_size - 1, 1),)),
        ],
        compiler_params=pltpu.CompilerParams(
            collective_id=0, has_side_effects=True, vmem_limit_bytes=24*2**20
        ),
    )(*[pltpu.with_memory_space_constraint(x, pltpu.HBM) for x in operands])
    reserve, block, capital = pl.pallas_call(
        settle,
        out_shape=[shape(reserve.shape, f32), shape(block.shape, f32), shape((1, 1), f32)],
        in_specs=[VMEM] * 3,
        out_specs=[pl.BlockSpec(memory_space=pltpu.HBM)] * 3,
        scratch_shapes=[buffer(1, 1), pltpu.SemaphoreType.DMA((3,))],
        compiler_params=pltpu.CompilerParams(vmem_limit_bytes=2**20),
    )(reserve, block, capital)
    return (
        reserve.reshape(2, kept, cells_local),
        block.reshape(2, kept, share),
        capital.reshape(1),
    )


def solution(mesh):
    placed = (
        P("outer", "cell"), P("outer", "cell"), P("outer", "cell"), P(), P("cell"), P("cell"), P("cell"),
        P("cell"), P("cell"), P("cell"), P("outer", "inner", None), P("outer", "inner", None),
        P("outer", None), P("outer"),
    )
    return jax.shard_map(
        body,
        mesh=mesh,
        in_specs=placed,
        out_specs=(P(None, ("outer", "inner"), "cell"), P(None, ("outer", "inner"), "cell"), P()),
        check_vma=False,
    )
```

```python
import functools
import jax
import jax.numpy as jnp
from jax import lax
from jax.experimental import pallas as pl
from jax.experimental.pallas import tpu as pltpu
from jax.sharding import PartitionSpec as P

PERIOD = 12
BLOCK = 128
LANES = 128
ROWS = 8
DIRECT = 32

credit_floor = 0.001
rollup_growth = 0.05
VMEM = pl.BlockSpec(memory_space=pltpu.VMEM)


def tiles(x, count):
    return jnp.concatenate([x] * count, axis=1)


def month(account, surviving, growth, nf, om, lb, keep, inverse):
    credited = jnp.maximum(account * keep + nf, 0.0) * growth
    lapse = lb * jnp.clip(credited * inverse, 0.5, 1.5)
    return credited, surviving * (om - lapse)


def claims_of(account, credited, surviving, guarantee, mf):
    return surviving * (mf * jnp.maximum(guarantee - credited, 0.0) - account)


def anniversary(account, guarantee, ratchet, rollup):
    return (
        guarantee
        + ratchet * (jnp.maximum(guarantee, account) - guarantee)
        + rollup * rollup_growth * guarantee
    )


def prefix(rates):
    months = rates.shape[1]
    tri = (
        lax.broadcasted_iota(jnp.int32, (months, months), 0)
        <= lax.broadcasted_iota(jnp.int32, (months, months), 1)
    ).astype(jnp.float32)
    return jnp.dot(rates, tri, precision=lax.Precision.HIGHEST, preferred_element_type=jnp.float32)


def spread_lanes(values, target, rows):
    for m in range(values.shape[1]):
        target[m, rows, :] = jnp.broadcast_to(values[:, m : m + 1], (values.shape[0], LANES))


def year(start, plans, cell, growth_lanes, first_month, state, width, begin, end):
    nf_ref, mf_ref, om_ref, lb_ref = plans
    repeat = width // LANES

    def chunk(j, _):
        cols = pl.ds(pl.multiple_of(j * width, width), width)
        account, surviving, guarantee = start(cols)
        keep, ratchet, rollup = cell[0:1, cols], cell[1:2, cols], cell[2:3, cols]
        inverse = 1.0 / guarantee
        for m in range(PERIOD):
            row = slice(first_month + m, first_month + m + 1)
            account, surviving = month(
                account,
                surviving,
                tiles(growth_lanes[m], repeat),
                nf_ref[row, cols],
                om_ref[row, cols],
                lb_ref[row, cols],
                keep,
                inverse,
            )
        state[0, :, cols] = account
        state[1, :, cols] = surviving
        state[2, :, cols] = anniversary(account, guarantee, ratchet, rollup)
        return 0

    lax.fori_loop(begin, end, chunk, 0)


def inner(state, plans, cell, gb, db, first_month, low, high, paths, sums, width, begin, end):
    nf_ref, mf_ref, om_ref, lb_ref = plans
    repeat = width // LANES
    months = db.shape[0]
    groups = paths // ROWS
    chunks = end - begin

    def block(step, _):
        o, j = low + step // chunks, begin + step % chunks
        cols = pl.ds(pl.multiple_of(j * width, width), width)
        keep, ratchet, rollup = cell[0:1, cols], cell[1:2, cols], cell[2:3, cols]
        shape = (ROWS, width)
        one = pl.ds(o, 1)
        account = [jnp.broadcast_to(state[0, one, cols], shape)] * groups
        surviving = [jnp.broadcast_to(state[1, one, cols], shape)] * groups
        guarantee = [jnp.broadcast_to(state[2, one, cols], shape)] * groups
        inverse = [1.0 / guarantee[0]] * groups
        rows = [pl.ds(pl.multiple_of(o * paths + g * ROWS, ROWS), ROWS) for g in range(groups)]
        present = jnp.zeros(shape, jnp.float32)
        for m in range(months):
            row = slice(first_month + m, first_month + m + 1)
            nf, mf, om, lb = nf_ref[row, cols], mf_ref[row, cols], om_ref[row, cols], lb_ref[row, cols]
            for g in range(groups):
                before, alive = account[g], surviving[g]
                account[g], surviving[g] = month(
                    before, alive, tiles(gb[m, rows[g], :], repeat), nf, om, lb, keep, inverse[g]
                )
                claims = claims_of(before, account[g], alive, guarantee[g], mf)
                present = present + tiles(db[m, rows[g], :], repeat) * claims
            if (m + 1) % PERIOD == 0 and m + 1 < months:
                for g in range(groups):
                    guarantee[g] = anniversary(account[g], guarantee[g], ratchet, rollup)
                    inverse[g] = 1.0 / guarantee[g]
        sums[o, :, cols] = present
        return 0

    lax.fori_loop(0, (high - low) * chunks, block, 0)


def reduce_rows(sums, out, low, high, scale):
    for o in range(low, high):
        out[o] = jnp.sum(sums[o], axis=0, keepdims=True) * scale


def fill_growth(rates_ref, spread_column, gb, low, high, paths):
    for o in range(low, high):
        for g in range(paths // ROWS):
            rows = slice(o * paths + g * ROWS, o * paths + (g + 1) * ROWS)
            spread_lanes(
                1.0 + jnp.maximum(rates_ref[rows, :] - spread_column[o : o + 1], credit_floor), gb, rows
            )


def fill_discount(rates_ref, db):
    discount = jnp.exp(-prefix(rates_ref[...]))
    for at in range(0, discount.shape[0], ROWS):
        spread_lanes(discount[at : at + ROWS], db, slice(at, at + ROWS))


def peers(axes):
    sizes = [lax.axis_size(axis) for axis in axes]
    count = 1
    place = 0
    for axis, size in zip(axes, sizes):
        place = place * size + lax.axis_index(axis)
        count *= size
    others = []
    for distance in range(1, count):
        index = lax.rem(place + distance, count)
        rest, device = index, {}
        for axis, size in reversed(list(zip(axes, sizes))):
            device[axis] = lax.rem(rest, size)
            rest = lax.div(rest, size)
        others.append((index, device))
    return place, others


def greet(groups):
    barrier = pltpu.get_barrier_semaphore()
    count = 0
    for others in groups:
        for _, device in others:
            pl.semaphore_signal(barrier, inc=1, device_id=device, device_id_type=pl.DeviceIdType.MESH)
            count += 1
    return barrier, count


def beside(me, size, act):
    @pl.when(me > 0)
    def _():
        act({"cell": me - 1})

    @pl.when(me < size - 1)
    def _():
        act({"cell": me + 1})

    return (me > 0).astype(jnp.int32) + (me < size - 1).astype(jnp.int32)


def signal_to(sem):
    def act(device):
        pl.semaphore_signal(sem, inc=1, device_id=device, device_id_type=pl.DeviceIdType.MESH)

    return act


def send(source, target, device, sems, at):
    copy = pltpu.make_async_remote_copy(
        src_ref=source,
        dst_ref=target,
        send_sem=sems.at[0, at],
        recv_sem=sems.at[1, at],
        device_id=device,
        device_id_type=pl.DeviceIdType.MESH,
    )
    copy.start()
    return copy


def finish(copies):
    for copy in copies:
        copy.wait()


def local_totals(partial, low, high):
    zero = jnp.zeros((1, LANES), jnp.float32)
    rows = [
        jnp.broadcast_to(jnp.sum(partial[o], axis=1, keepdims=True), (1, LANES)) if low <= o < high else zero
        for o in range(ROWS)
    ]
    return jnp.concatenate(rows, axis=0)


def whole_kernel(
    outers, paths, paths_all, cells_all, width,
    premium, charge, mortality, table_in, lapse_in, type_in, block_in, account_in, guarantee_in, fee_in,
    first_in, second_in, world_in, spread_in,
    reserve, block, capital,
    v_premium, v_charge, table, lapse, kind, block_row, account, guarantee, fee,
    first_rates, second_rates, world, spread,
    nf_all, mort_all, nf_ref, mf_ref, om_ref, lb_ref, cell, state_one, state_two,
    gb, db_one, db_two, gw, sums, first, second,
    slots_one, slots_two, kept_slots, hot, term_slots, term_out, loss_slots,
    load_sems, plan_sems, pass_sems, one_sems, total_sems, kept_sems, term_sems, loss_sems, relay_sems,
):
    outer_size, months_local, cells_local = nf_all.shape
    inner_size = kept_slots.shape[1]
    cell_size = term_out.shape[0]
    kept = reserve.shape[1]
    blocks = hot.shape[0]
    share = block.shape[3]
    group, group_others = peers(("inner", "cell"))
    inner_me, inner_others = peers(("inner",))
    cell_me, cell_others = peers(("cell",))
    outer_me, outer_others = peers(("outer",))
    direct = slots_two.shape[0] > inner_size * cell_size
    all_me, all_others = peers(("outer", "inner", "cell")) if direct else (group, group_others)
    barrier, arrivals = greet([inner_others, outer_others])
    arrivals = arrivals + beside(cell_me, cell_size, signal_to(barrier))
    loads = [
        pltpu.make_async_copy(source, target, load_sems.at[i])
        for i, (source, target) in enumerate(
            [
                (premium, v_premium), (charge, v_charge), (mortality, mort_all.at[outer_me]),
                (table_in, table), (lapse_in, lapse), (type_in, kind), (block_in, block_row),
                (account_in, account), (guarantee_in, guarantee), (fee_in, fee),
                (first_in, first_rates), (second_in, second_rates), (world_in, world), (spread_in, spread),
            ]
        )
    ]
    for copy in loads:
        copy.start()
    finish(loads[:3])
    nf_all[outer_me] = v_premium[...] - v_charge[...]
    pl.semaphore_wait(barrier, arrivals)

    pair = inner_size % 2 == 0
    chunks = cells_local // width
    part = width // 2 if pair else width
    side = lax.rem(inner_me, 2) if pair else 0
    plan_copies = []
    for j in range(chunks):
        mine = pl.ds(pl.multiple_of(j * width + side * part, part), part)
        copies = []
        for d, (_, device) in enumerate(outer_others):
            for k, plan in enumerate((nf_all, mort_all)):
                piece = plan.at[outer_me, :, mine]
                slot = (j * len(outer_others) + d) * 2 + k
                copies.append((d, plan, mine, slot, send(piece, piece, device, plan_sems, slot)))
        plan_copies.append(copies)
    pass_copies = []

    def pass_on(j):
        copies = []
        for d, plan, mine, slot, copy in plan_copies[j]:
            copy.wait_recv()
            if pair:
                source = lax.rem(outer_me + outer_size - 1 - d, outer_size)
                piece = plan.at[source, :, mine]
                partner = {"inner": inner_me + 1 - 2 * side}
                copies.append(send(piece, piece, partner, pass_sems, slot))
        pass_copies.append(copies)

    rounds = relay_sems.shape[0]

    def relay(low, high):
        for r in range(low, min(high, rounds)):
            pl.semaphore_wait(relay_sems.at[r - 1], near)
            beside(cell_me, cell_size, signal_to(relay_sems.at[r]))

    near = beside(cell_me, cell_size, signal_to(relay_sems.at[0]))
    finish(loads[3:])
    fee_row = fee[...]
    cell[0:1, :] = 1.0 - fee_row
    cell[1:2, :] = (kind[...] == 1).astype(jnp.float32)
    cell[2:3, :] = (kind[...] == 2).astype(jnp.float32)
    lapse_hot = (
        lax.broadcasted_iota(jnp.int32, (table.shape[0], cells_local), 0) == lapse[...]
    ).astype(jnp.float32)
    lb_ref[...] = lax.dot_general(
        table[...], lapse_hot, (((0,), (0,)), ((), ())),
        precision=lax.Precision.HIGHEST, preferred_element_type=jnp.float32,
    )
    world_rows = jnp.concatenate(
        [world[...], jnp.zeros((ROWS - outers, world.shape[1]), jnp.float32)], axis=0
    )
    diagonal = lax.broadcasted_iota(jnp.int32, (ROWS, outers), 0) == lax.broadcasted_iota(
        jnp.int32, (ROWS, outers), 1
    )
    spread_one = jnp.sum(jnp.where(diagonal, spread[...], 0.0), axis=1, keepdims=True)
    everything = slice(0, ROWS)
    spread_lanes(1.0 + jnp.maximum(world_rows[:, :PERIOD] - spread_one, credit_floor), gw, everything)
    fill_growth(first_rates, spread_one, gb, 0, outers, paths)
    fill_discount(first_rates, db_one)
    fill_discount(second_rates, db_two)
    hot[...] = (
        lax.broadcasted_iota(jnp.int32, (blocks, cells_local), 0) == block_row[...]
    ).astype(jnp.float32).astype(jnp.bfloat16)
    ahead = min(2, chunks)
    for j in range(ahead):
        pass_on(j)
    relay(1, 2)
    death = 1.0 / fee_row
    plans = (nf_ref, mf_ref, om_ref, lb_ref)

    def prepare(j):
        for copy in pass_copies[j]:
            copy.wait_recv()
        cols = slice(j * width, (j + 1) * width)
        for s in range(outer_size):
            rows = slice(s * months_local, (s + 1) * months_local)
            nf_ref[rows, cols] = nf_all[s, :, cols] * fee_row[:, cols]
            mf_ref[rows, cols] = mort_all[s, :, cols] * death[:, cols]
            om_ref[rows, cols] = 1.0 - mort_all[s, :, cols]

    def start_one(cols):
        scale = fee[0:1, cols]
        shape = (ROWS, width)
        return (
            jnp.broadcast_to(account[0:1, cols] * scale, shape),
            jnp.ones(shape, jnp.float32),
            jnp.broadcast_to(guarantee[0:1, cols] * scale, shape),
        )

    def start_two(cols):
        return state_one[0, :, cols], state_one[1, :, cols], state_one[2, :, cols]

    split = -(-outers // 2)
    halves = [(low, high) for low, high in ((0, split), (split, outers)) if low < high]
    distances = len(group_others)
    one_copies = []
    for h, (low, high) in enumerate(halves):
        if h == 0:
            for j in range(chunks):
                prepare(j)
                year(start_one, plans, cell, gw, 0, state_one, width, j, j + 1)
                inner(state_one, plans, cell, gb, db_one, PERIOD, low, high, paths, sums, width, j, j + 1)
                if j == 0:
                    for later in range(ahead, chunks):
                        pass_on(later)
                    relay(2, rounds)
        else:
            inner(state_one, plans, cell, gb, db_one, PERIOD, low, high, paths, sums, width, 0, chunks)
        reduce_rows(sums, first, low, high, 1.0 / paths_all)
        slots_one[h, group] = local_totals(first, low, high)
        if h == 0:
            for copies in plan_copies:
                for piece in copies:
                    piece[4].wait_send()
            for copies in pass_copies:
                for copy in copies:
                    copy.wait_send()
            pl.semaphore_wait(relay_sems.at[rounds - 1], near)
        slot = slots_one.at[h, group]
        one_copies.append(
            [
                send(slot, slot, device, one_sems, h * distances + d)
                for d, (_, device) in enumerate(group_others)
            ]
        )
    kept_copies = []

    def send_kept(date, partial):
        for index, device in inner_others:
            kept_copies.append(
                send(
                    partial.at[pl.ds(index * kept, kept)], kept_slots.at[date, inner_me],
                    device, kept_sems, len(kept_copies),
                )
            )
        kept_slots[date, inner_me] = partial[pl.ds(inner_me * kept, kept)]

    send_kept(0, first)
    total_one = jnp.zeros((ROWS, LANES), jnp.float32)
    for h, (low, high) in enumerate(halves):
        finish(one_copies[h])
        total_one = total_one + jnp.sum(slots_one[h], axis=0)
        spread_two = (spread_one * (1.0 + jnp.tanh(total_one / cells_all)))[:, 0:1]
        spread_lanes(1.0 + jnp.maximum(world_rows[:, PERIOD:] - spread_two, credit_floor), gw, everything)
        year(start_two, plans, cell, gw, PERIOD, state_two, width, 0, chunks)
        fill_growth(second_rates, spread_two, gb, low, high, paths)
        inner(state_two, plans, cell, gb, db_two, 2 * PERIOD, low, high, paths, sums, width, 0, chunks)
        reduce_rows(sums, second, low, high, 1.0 / paths_all)
    discount = jnp.exp(-jnp.sum(world_rows[:, PERIOD:], axis=1, keepdims=True))
    mine_one = slots_one[0, group]
    for h in range(1, len(halves)):
        mine_one = mine_one + slots_one[h, group]
    mine_loss = (discount * local_totals(second, 0, outers) - mine_one) / cells_all
    own = lax.broadcasted_iota(jnp.int32, (ROWS, LANES), 0)
    own_lane = lax.broadcasted_iota(jnp.int32, (ROWS, LANES), 1) - outer_me * outers
    mine_loss = jnp.where((own == own_lane) & (own < outers), mine_loss, 0.0)
    place, others = (all_me, all_others) if direct else (group, group_others)
    slots_two[place] = jnp.sum(mine_loss, axis=0, keepdims=True)
    total_copies = [
        send(slots_two.at[place], slots_two.at[place], device, total_sems, d)
        for d, (_, device) in enumerate(others)
    ]
    send_kept(1, second)
    step = -(-outers // ROWS) * ROWS
    lines = 2 * step
    line = lax.broadcasted_iota(jnp.int32, (step, cells_local), 0)
    values = []
    for partial in (first, second):
        value = jnp.zeros((step, cells_local), jnp.float32)
        for o in range(outers):
            value = jnp.where(line == o, jnp.broadcast_to(partial[o], value.shape), value)
        values.append(value)
    value = jnp.concatenate(values, axis=0)
    high = value.astype(jnp.bfloat16).astype(jnp.float32)
    value = value - high
    middle = value.astype(jnp.bfloat16).astype(jnp.float32)
    stacked = jnp.concatenate([high, middle, value - middle], axis=0)
    products = lax.dot_general(
        stacked.astype(jnp.bfloat16), hot[...], (((1,), (1,)), ((), ())),
        preferred_element_type=jnp.float32,
    )
    terms = products[:lines] + products[lines : 2 * lines] + products[2 * lines :]
    width = term_out.shape[3]
    for k in range(cell_size):
        spot = slice(k * share, (k + 1) * share)
        part = [terms[:step, spot], terms[step:, spot]]
        if width > 2 * share:
            part.append(jnp.zeros((step, width - 2 * share), jnp.float32))
        part = jnp.concatenate(part, axis=1)
        for o in range(outers):
            term_out[k, o] = part[o : o + 1]
    term_slots[group] = term_out[cell_me, pl.ds(inner_me * kept, kept)]
    term_copies = [
        send(
            term_out.at[lax.rem(index, cell_size), pl.ds(lax.div(index, cell_size) * kept, kept)],
            term_slots.at[group], device, term_sems, d,
        )
        for d, (index, device) in enumerate(group_others)
    ]
    finish(kept_copies)
    for date in range(2):
        for q in range(kept):
            reserve[date, q] = jnp.sum(kept_slots[date, :, q], axis=0)
    finish(term_copies)
    for q in range(kept):
        mine = jnp.sum(term_slots[:, q], axis=0)
        for date in range(2):
            block[date, q] = mine[:, date * share : (date + 1) * share]
    finish(total_copies)
    across = jnp.sum(slots_two[...], axis=0)
    if not direct:
        loss_slots[outer_me] = across
        finish(
            [
                send(loss_slots.at[outer_me], loss_slots.at[outer_me], device, loss_sems, d)
                for d, (_, device) in enumerate(outer_others)
            ]
        )
        across = jnp.sum(loss_slots[...], axis=0)
    count = outers * outer_size
    lane = lax.broadcasted_iota(jnp.int32, (count, LANES), 1)
    row = lax.broadcasted_iota(jnp.int32, (count, LANES), 0)
    losses = jnp.sum(jnp.where(lane == row, across, 0.0), axis=1, keepdims=True)
    ahead = ((across > losses) | ((across == losses) & (lane < row))) & (lane < count)
    rank = jnp.sum(jnp.where(ahead, 1.0, 0.0), axis=1, keepdims=True)
    top = count // 4
    taken = jnp.sum(jnp.where(rank < top, losses, 0.0), axis=0, keepdims=True) / top
    capital[...] = jnp.broadcast_to(taken, capital.shape)


def settle(reserve, block, capital, reserve_out, block_out, capital_out, single, sems):
    single[...] = capital[:, :1]
    copies = [
        pltpu.make_async_copy(source, target, sems.at[i])
        for i, (source, target) in enumerate(
            [(reserve, reserve_out), (block, block_out), (single, capital_out)]
        )
    ]
    for copy in copies:
        copy.start()
    finish(copies)


def body(
    premium, charge, mortality, lapse_table, lapse_index, guarantee_type, block_index,
    account_start, guarantee_start, fee_rate, first_rates, second_rates, world_rates, spread,
):
    months_local, cells_local = premium.shape
    outer_size, inner_size, cell_size = (lax.axis_size(axis) for axis in ("outer", "inner", "cell"))
    months = months_local * outer_size
    group_size = inner_size * cell_size
    outers, paths = first_rates.shape[:2]
    paths_all = paths * inner_size
    cells_all = cells_local * cell_size
    width = 4 * LANES
    kept = outers // inner_size
    blocks = 4 * cells_all // BLOCK
    share = blocks // cell_size
    wide = -(-2 * share // LANES) * LANES
    everyone = outer_size * group_size
    wide_count = everyone if everyone <= DIRECT else group_size
    f32, i32 = jnp.float32, jnp.int32
    shape = jax.ShapeDtypeStruct

    def row(x):
        return x.reshape(1, -1)

    def buffer(*dims, dtype=f32):
        return pltpu.VMEM(dims, dtype)

    def sems(count):
        return pltpu.SemaphoreType.DMA((2, max(count, 1)))

    chunks = cells_local // width
    plan_count = 2 * chunks * (outer_size - 1)
    plan = buffer(months, cells_local)
    gathered = buffer(outer_size, months_local, cells_local)
    line, code = buffer(1, cells_local), buffer(1, cells_local, dtype=i32)
    total_rows = outers * paths
    first_months, second_months = first_rates.shape[2], second_rates.shape[2]
    operands = (
        premium, charge, mortality, lapse_table, row(lapse_index), row(guarantee_type), row(block_index),
        row(account_start), row(guarantee_start), row(fee_rate),
        first_rates.reshape(total_rows, -1), second_rates.reshape(total_rows, -1), world_rates, row(spread),
    )
    reserve, block, capital = pl.pallas_call(
        functools.partial(whole_kernel, outers, paths, paths_all, cells_all, width),
        out_shape=[
            shape((2, kept, 1, cells_local), f32), shape((2, kept, 1, share), f32), shape((1, LANES), f32),
        ],
        in_specs=[pl.BlockSpec(memory_space=pl.ANY)] * len(operands),
        out_specs=[VMEM] * 3,
        scratch_shapes=[
            buffer(months_local, cells_local), buffer(months_local, cells_local), buffer(*lapse_table.shape),
            code, code, code, line, line, line,
            buffer(total_rows, first_months), buffer(total_rows, second_months),
            buffer(*world_rates.shape), buffer(1, outers),
            gathered, gathered, plan, plan, plan, plan, buffer(ROWS, cells_local),
            buffer(3, ROWS, cells_local), buffer(3, ROWS, cells_local),
            buffer(first_months, total_rows, LANES), buffer(first_months, total_rows, LANES),
            buffer(second_months, total_rows, LANES), buffer(PERIOD, ROWS, LANES),
            buffer(outers, ROWS, cells_local), buffer(outers, 1, cells_local), buffer(outers, 1, cells_local),
            buffer(2, group_size, ROWS, LANES), buffer(wide_count, 1, LANES),
            buffer(2, inner_size, kept, 1, cells_local), buffer(blocks, cells_local, dtype=jnp.bfloat16),
            buffer(group_size, kept, 1, wide), buffer(cell_size, outers, 1, wide),
            buffer(outer_size, 1, LANES),
            pltpu.SemaphoreType.DMA((len(operands),)), sems(plan_count), sems(plan_count),
            sems(2 * (group_size - 1)), sems(wide_count - 1), sems(2 * (inner_size - 1)),
            sems(group_size - 1), sems(outer_size - 1), pltpu.SemaphoreType.REGULAR((max(cell_size - 1, 1),)),
        ],
        compiler_params=pltpu.CompilerParams(
            collective_id=0, has_side_effects=True, vmem_limit_bytes=24*2**20
        ),
    )(*[pltpu.with_memory_space_constraint(x, pltpu.HBM) for x in operands])
    reserve, block, capital = pl.pallas_call(
        settle,
        out_shape=[shape(reserve.shape, f32), shape(block.shape, f32), shape((1, 1), f32)],
        in_specs=[VMEM] * 3,
        out_specs=[pl.BlockSpec(memory_space=pltpu.HBM)] * 3,
        scratch_shapes=[buffer(1, 1), pltpu.SemaphoreType.DMA((3,))],
        compiler_params=pltpu.CompilerParams(vmem_limit_bytes=2**20),
    )(reserve, block, capital)
    return (
        reserve.reshape(2, kept, cells_local),
        block.reshape(2, kept, share),
        capital.reshape(1),
    )


def solution(mesh):
    placed = (
        P("outer", "cell"), P("outer", "cell"), P("outer", "cell"), P(), P("cell"), P("cell"), P("cell"),
        P("cell"), P("cell"), P("cell"), P("outer", "inner", None), P("outer", "inner", None),
        P("outer", None), P("outer"),
    )
    return jax.shard_map(
        body,
        mesh=mesh,
        in_specs=placed,
        out_specs=(P(None, ("outer", "inner"), "cell"), P(None, ("outer", "inner"), "cell"), P()),
        check_vma=False,
    )
```

```python
import functools
import jax
import jax.numpy as jnp
from jax import lax
from jax.experimental import pallas as pl
from jax.experimental.pallas import tpu as pltpu
from jax.sharding import PartitionSpec as P

PERIOD = 12
BLOCK = 128
LANES = 128
ROWS = 8
DIRECT = 32

credit_floor = 0.001
rollup_growth = 0.05
VMEM = pl.BlockSpec(memory_space=pltpu.VMEM)


def tiles(x, count):
    return jnp.concatenate([x] * count, axis=1)


def month(account, surviving, growth, nf, om, lb, keep, inverse):
    credited = jnp.maximum(account * keep + nf, 0.0) * growth
    lapse = lb * jnp.clip(credited * inverse, 0.5, 1.5)
    return credited, surviving * (om - lapse)


def claims_of(account, credited, surviving, guarantee, mf):
    return surviving * (mf * jnp.maximum(guarantee - credited, 0.0) - account)


def anniversary(account, guarantee, ratchet, rollup):
    return (
        guarantee
        + ratchet * (jnp.maximum(guarantee, account) - guarantee)
        + rollup * rollup_growth * guarantee
    )


def prefix(rates):
    months = rates.shape[1]
    tri = (
        lax.broadcasted_iota(jnp.int32, (months, months), 0)
        <= lax.broadcasted_iota(jnp.int32, (months, months), 1)
    ).astype(jnp.float32)
    return jnp.dot(rates, tri, precision=lax.Precision.HIGHEST, preferred_element_type=jnp.float32)


def spread_lanes(values, target, rows):
    for m in range(values.shape[1]):
        target[m, rows, :] = jnp.broadcast_to(values[:, m : m + 1], (values.shape[0], LANES))


def year(start, plans, cell, growth_lanes, first_month, state, width, begin, end):
    nf_ref, mf_ref, om_ref, lb_ref = plans
    repeat = width // LANES

    def chunk(j, _):
        cols = pl.ds(pl.multiple_of(j * width, width), width)
        account, surviving, guarantee = start(cols)
        keep, ratchet, rollup = cell[0:1, cols], cell[1:2, cols], cell[2:3, cols]
        inverse = 1.0 / guarantee
        for m in range(PERIOD):
            row = slice(first_month + m, first_month + m + 1)
            account, surviving = month(
                account,
                surviving,
                tiles(growth_lanes[m], repeat),
                nf_ref[row, cols],
                om_ref[row, cols],
                lb_ref[row, cols],
                keep,
                inverse,
            )
        state[0, :, cols] = account
        state[1, :, cols] = surviving
        state[2, :, cols] = anniversary(account, guarantee, ratchet, rollup)
        return 0

    lax.fori_loop(begin, end, chunk, 0)


def inner(state, plans, cell, gb, db, first_month, low, high, paths, sums, width, begin, end, flows):
    nf_ref, mf_ref, om_ref, lb_ref = plans
    repeat = width // LANES
    months = db.shape[0]
    groups = paths // ROWS
    chunks = end - begin
    base = first_month // ROWS * ROWS
    top = -(-(first_month + PERIOD) // ROWS) * ROWS

    def block(step, _):
        o, j = low + step // chunks, begin + step % chunks
        cols = pl.ds(pl.multiple_of(j * width, width), width)
        keep, ratchet, rollup = cell[0:1, cols], cell[1:2, cols], cell[2:3, cols]
        shape = (ROWS, width)
        one = pl.ds(o, 1)
        guarantee = state[2, one, cols]
        across = 1.0 / guarantee
        flows[: top - base, :] = nf_ref[base:top, cols] * across
        ratio = [jnp.broadcast_to(state[0, one, cols] * across, shape)] * groups
        weight = [jnp.broadcast_to(state[1, one, cols] * guarantee, shape)] * groups
        inverse = [jnp.broadcast_to(across, shape)] * groups
        rows = [pl.ds(pl.multiple_of(o * paths + g * ROWS, ROWS), ROWS) for g in range(groups)]
        present = jnp.zeros(shape, jnp.float32)
        for m in range(months):
            row = slice(first_month + m, first_month + m + 1)
            mf, om, lb = mf_ref[row, cols], om_ref[row, cols], lb_ref[row, cols]
            for g in range(groups):
                if m < PERIOD:
                    at = first_month - base + m
                    nf = flows[at : at + 1, :]
                else:
                    nf = nf_ref[row, cols] * inverse[g]
                before, alive = ratio[g], weight[g]
                after = jnp.maximum(before * keep + nf, 0.0) * tiles(gb[m, rows[g], :], repeat)
                weight[g] = alive * (om - lb * jnp.clip(after, 0.5, 1.5))
                claims = alive * (mf * jnp.maximum(1.0 - after, 0.0) - before)
                present = present + tiles(db[m, rows[g], :], repeat) * claims
                ratio[g] = after
            if (m + 1) % PERIOD == 0 and m + 1 < months:
                for g in range(groups):
                    lift = 1.0 + ratchet * (jnp.maximum(ratio[g], 1.0) - 1.0) + rollup * rollup_growth
                    drop = 1.0 / lift
                    ratio[g] = ratio[g] * drop
                    weight[g] = weight[g] * lift
                    inverse[g] = inverse[g] * drop
        sums[o, :, cols] = present
        return 0

    lax.fori_loop(0, (high - low) * chunks, block, 0)


def reduce_rows(sums, out, low, high, scale):
    for o in range(low, high):
        out[o] = jnp.sum(sums[o], axis=0, keepdims=True) * scale


def fill_growth(rates_ref, spread_column, gb, low, high, paths):
    for o in range(low, high):
        for g in range(paths // ROWS):
            rows = slice(o * paths + g * ROWS, o * paths + (g + 1) * ROWS)
            spread_lanes(
                1.0 + jnp.maximum(rates_ref[rows, :] - spread_column[o : o + 1], credit_floor), gb, rows
            )


def fill_later_growth(rates_lanes, spread_column, gb, low, high, paths):
    for o in range(low, high):
        rows = slice(o * paths, (o + 1) * paths)
        less = jnp.broadcast_to(spread_column[o : o + 1], (paths, LANES))
        for m in range(rates_lanes.shape[0]):
            gb[m, rows, :] = 1.0 + jnp.maximum(rates_lanes[m, rows, :] - less, credit_floor)


def fill_discount(rates_ref, db):
    discount = jnp.exp(-prefix(rates_ref[...]))
    for at in range(0, discount.shape[0], ROWS):
        spread_lanes(discount[at : at + ROWS], db, slice(at, at + ROWS))


def peers(axes):
    sizes = [lax.axis_size(axis) for axis in axes]
    count = 1
    place = 0
    for axis, size in zip(axes, sizes):
        place = place * size + lax.axis_index(axis)
        count *= size
    others = []
    for distance in range(1, count):
        index = lax.rem(place + distance, count)
        rest, device = index, {}
        for axis, size in reversed(list(zip(axes, sizes))):
            device[axis] = lax.rem(rest, size)
            rest = lax.div(rest, size)
        others.append((index, device))
    return place, others


def greet(groups):
    barrier = pltpu.get_barrier_semaphore()
    count = 0
    for others in groups:
        for _, device in others:
            pl.semaphore_signal(barrier, inc=1, device_id=device, device_id_type=pl.DeviceIdType.MESH)
            count += 1
    return barrier, count


def beside(me, size, act):
    @pl.when(me > 0)
    def _():
        act({"cell": me - 1})

    @pl.when(me < size - 1)
    def _():
        act({"cell": me + 1})

    return (me > 0).astype(jnp.int32) + (me < size - 1).astype(jnp.int32)


def signal_to(sem):
    def act(device):
        pl.semaphore_signal(sem, inc=1, device_id=device, device_id_type=pl.DeviceIdType.MESH)

    return act


def send(source, target, device, sems, at):
    copy = pltpu.make_async_remote_copy(
        src_ref=source,
        dst_ref=target,
        send_sem=sems.at[0, at],
        recv_sem=sems.at[1, at],
        device_id=device,
        device_id_type=pl.DeviceIdType.MESH,
    )
    copy.start()
    return copy


def finish(copies):
    for copy in copies:
        copy.wait()


def local_totals(partial, low, high):
    zero = jnp.zeros((1, LANES), jnp.float32)
    rows = [
        jnp.broadcast_to(jnp.sum(partial[o], axis=1, keepdims=True), (1, LANES)) if low <= o < high else zero
        for o in range(ROWS)
    ]
    return jnp.concatenate(rows, axis=0)


def whole_kernel(
    outers, paths, paths_all, cells_all, width,
    premium, charge, mortality, table_in, lapse_in, type_in, block_in, account_in, guarantee_in, fee_in,
    first_in, second_in, world_in, spread_in,
    reserve, block, capital,
    v_premium, v_charge, table, lapse, kind, block_row, account, guarantee, fee,
    first_rates, second_rates, world, spread,
    nf_all, mort_all, nf_ref, mf_ref, om_ref, lb_ref, cell, state_one, state_two,
    gb, db_one, db_two, rb_two, flows, gw, sums, first, second,
    slots_one, slots_two, kept_slots, hot, term_slots, term_out, loss_slots,
    load_sems, plan_sems, pass_sems, one_sems, total_sems, kept_sems, term_sems, loss_sems, relay_sems,
):
    outer_size, months_local, cells_local = nf_all.shape
    inner_size = kept_slots.shape[1]
    cell_size = term_out.shape[0]
    kept = reserve.shape[1]
    blocks = hot.shape[0]
    share = block.shape[3]
    group, group_others = peers(("inner", "cell"))
    inner_me, inner_others = peers(("inner",))
    cell_me, cell_others = peers(("cell",))
    outer_me, outer_others = peers(("outer",))
    direct = slots_two.shape[0] > inner_size * cell_size
    all_me, all_others = peers(("outer", "inner", "cell")) if direct else (group, group_others)
    barrier, arrivals = greet([inner_others, outer_others])
    arrivals = arrivals + beside(cell_me, cell_size, signal_to(barrier))
    loads = [
        pltpu.make_async_copy(source, target, load_sems.at[i])
        for i, (source, target) in enumerate(
            [
                (premium, v_premium), (charge, v_charge), (mortality, mort_all.at[outer_me]),
                (table_in, table), (lapse_in, lapse), (type_in, kind), (block_in, block_row),
                (account_in, account), (guarantee_in, guarantee), (fee_in, fee),
                (first_in, first_rates), (second_in, second_rates), (world_in, world), (spread_in, spread),
            ]
        )
    ]
    for copy in loads:
        copy.start()
    finish(loads[:3])
    nf_all[outer_me] = v_premium[...] - v_charge[...]
    pl.semaphore_wait(barrier, arrivals)

    pair = inner_size % 2 == 0
    chunks = cells_local // width
    part = width // 2 if pair else width
    side = lax.rem(inner_me, 2) if pair else 0
    plan_copies = []
    for j in range(chunks):
        mine = pl.ds(pl.multiple_of(j * width + side * part, part), part)
        copies = []
        for d, (_, device) in enumerate(outer_others):
            for k, plan in enumerate((nf_all, mort_all)):
                piece = plan.at[outer_me, :, mine]
                slot = (j * len(outer_others) + d) * 2 + k
                copies.append((d, plan, mine, slot, send(piece, piece, device, plan_sems, slot)))
        plan_copies.append(copies)
    pass_copies = []

    def pass_on(j):
        copies = []
        for d, plan, mine, slot, copy in plan_copies[j]:
            copy.wait_recv()
            if pair:
                source = lax.rem(outer_me + outer_size - 1 - d, outer_size)
                piece = plan.at[source, :, mine]
                partner = {"inner": inner_me + 1 - 2 * side}
                copies.append(send(piece, piece, partner, pass_sems, slot))
        pass_copies.append(copies)

    rounds = relay_sems.shape[0]

    def relay(low, high):
        for r in range(low, min(high, rounds)):
            pl.semaphore_wait(relay_sems.at[r - 1], near)
            beside(cell_me, cell_size, signal_to(relay_sems.at[r]))

    near = beside(cell_me, cell_size, signal_to(relay_sems.at[0]))
    finish(loads[3:])
    fee_row = fee[...]
    cell[0:1, :] = 1.0 - fee_row
    cell[1:2, :] = (kind[...] == 1).astype(jnp.float32)
    cell[2:3, :] = (kind[...] == 2).astype(jnp.float32)
    lapse_hot = (
        lax.broadcasted_iota(jnp.int32, (table.shape[0], cells_local), 0) == lapse[...]
    ).astype(jnp.float32)
    lb_ref[...] = lax.dot_general(
        table[...], lapse_hot, (((0,), (0,)), ((), ())),
        precision=lax.Precision.HIGHEST, preferred_element_type=jnp.float32,
    )
    world_rows = jnp.concatenate(
        [world[...], jnp.zeros((ROWS - outers, world.shape[1]), jnp.float32)], axis=0
    )
    diagonal = lax.broadcasted_iota(jnp.int32, (ROWS, outers), 0) == lax.broadcasted_iota(
        jnp.int32, (ROWS, outers), 1
    )
    spread_one = jnp.sum(jnp.where(diagonal, spread[...], 0.0), axis=1, keepdims=True)
    everything = slice(0, ROWS)
    spread_lanes(1.0 + jnp.maximum(world_rows[:, :PERIOD] - spread_one, credit_floor), gw, everything)
    fill_growth(first_rates, spread_one, gb, 0, outers, paths)
    fill_discount(first_rates, db_one)
    fill_discount(second_rates, db_two)
    for at in range(0, second_rates.shape[0], ROWS):
        spread_lanes(second_rates[at : at + ROWS, :], rb_two, slice(at, at + ROWS))
    hot[...] = (
        lax.broadcasted_iota(jnp.int32, (blocks, cells_local), 0) == block_row[...]
    ).astype(jnp.float32).astype(jnp.bfloat16)
    ahead = min(2, chunks)
    for j in range(ahead):
        pass_on(j)
    relay(1, 2)
    death = 1.0 / fee_row
    plans = (nf_ref, mf_ref, om_ref, lb_ref)

    def prepare(j):
        for copy in pass_copies[j]:
            copy.wait_recv()
        cols = slice(j * width, (j + 1) * width)
        for s in range(outer_size):
            rows = slice(s * months_local, (s + 1) * months_local)
            nf_ref[rows, cols] = nf_all[s, :, cols] * fee_row[:, cols]
            mf_ref[rows, cols] = mort_all[s, :, cols] * death[:, cols]
            om_ref[rows, cols] = 1.0 - mort_all[s, :, cols]

    def start_one(cols):
        scale = fee[0:1, cols]
        shape = (ROWS, width)
        return (
            jnp.broadcast_to(account[0:1, cols] * scale, shape),
            jnp.ones(shape, jnp.float32),
            jnp.broadcast_to(guarantee[0:1, cols] * scale, shape),
        )

    def start_two(cols):
        return state_one[0, :, cols], state_one[1, :, cols], state_one[2, :, cols]

    split = -(-outers // 2)
    halves = [(low, high) for low, high in ((0, split), (split, outers)) if low < high]
    distances = len(group_others)
    one_copies = []
    for h, (low, high) in enumerate(halves):
        if h == 0:
            for j in range(chunks):
                prepare(j)
                year(start_one, plans, cell, gw, 0, state_one, width, j, j + 1)
                inner(state_one, plans, cell, gb, db_one, PERIOD, low, high, paths, sums, width, j, j + 1, flows)
                if j == 0:
                    for later in range(ahead, chunks):
                        pass_on(later)
                    relay(2, rounds)
        else:
            inner(state_one, plans, cell, gb, db_one, PERIOD, low, high, paths, sums, width, 0, chunks, flows)
        reduce_rows(sums, first, low, high, 1.0 / paths_all)
        slots_one[h, group] = local_totals(first, low, high)
        if h == 0:
            for copies in plan_copies:
                for piece in copies:
                    piece[4].wait_send()
            for copies in pass_copies:
                for copy in copies:
                    copy.wait_send()
            pl.semaphore_wait(relay_sems.at[rounds - 1], near)
        slot = slots_one.at[h, group]
        one_copies.append(
            [
                send(slot, slot, device, one_sems, h * distances + d)
                for d, (_, device) in enumerate(group_others)
            ]
        )
    kept_copies = []

    def send_kept(date, partial):
        for index, device in inner_others:
            kept_copies.append(
                send(
                    partial.at[pl.ds(index * kept, kept)], kept_slots.at[date, inner_me],
                    device, kept_sems, len(kept_copies),
                )
            )
        kept_slots[date, inner_me] = partial[pl.ds(inner_me * kept, kept)]

    send_kept(0, first)
    total_one = jnp.zeros((ROWS, LANES), jnp.float32)
    for h, (low, high) in enumerate(halves):
        finish(one_copies[h])
        total_one = total_one + jnp.sum(slots_one[h], axis=0)
        spread_two = (spread_one * (1.0 + jnp.tanh(total_one / cells_all)))[:, 0:1]
        spread_lanes(1.0 + jnp.maximum(world_rows[:, PERIOD:] - spread_two, credit_floor), gw, everything)
        year(start_two, plans, cell, gw, PERIOD, state_two, width, 0, chunks)
        fill_later_growth(rb_two, spread_two, gb, low, high, paths)
        inner(state_two, plans, cell, gb, db_two, 2 * PERIOD, low, high, paths, sums, width, 0, chunks, flows)
        reduce_rows(sums, second, low, high, 1.0 / paths_all)
    discount = jnp.exp(-jnp.sum(world_rows[:, PERIOD:], axis=1, keepdims=True))
    mine_one = slots_one[0, group]
    for h in range(1, len(halves)):
        mine_one = mine_one + slots_one[h, group]
    mine_loss = (discount * local_totals(second, 0, outers) - mine_one) / cells_all
    own = lax.broadcasted_iota(jnp.int32, (ROWS, LANES), 0)
    own_lane = lax.broadcasted_iota(jnp.int32, (ROWS, LANES), 1) - outer_me * outers
    mine_loss = jnp.where((own == own_lane) & (own < outers), mine_loss, 0.0)
    place, others = (all_me, all_others) if direct else (group, group_others)
    slots_two[place] = jnp.sum(mine_loss, axis=0, keepdims=True)
    total_copies = [
        send(slots_two.at[place], slots_two.at[place], device, total_sems, d)
        for d, (_, device) in enumerate(others)
    ]
    send_kept(1, second)
    step = -(-outers // ROWS) * ROWS
    lines = 2 * step
    line = lax.broadcasted_iota(jnp.int32, (step, cells_local), 0)
    values = []
    for partial in (first, second):
        value = jnp.zeros((step, cells_local), jnp.float32)
        for o in range(outers):
            value = jnp.where(line == o, jnp.broadcast_to(partial[o], value.shape), value)
        values.append(value)
    value = jnp.concatenate(values, axis=0)
    high = value.astype(jnp.bfloat16).astype(jnp.float32)
    value = value - high
    middle = value.astype(jnp.bfloat16).astype(jnp.float32)
    stacked = jnp.concatenate([high, middle, value - middle], axis=0)
    products = lax.dot_general(
        stacked.astype(jnp.bfloat16), hot[...], (((1,), (1,)), ((), ())),
        preferred_element_type=jnp.float32,
    )
    terms = products[:lines] + products[lines : 2 * lines] + products[2 * lines :]
    width = term_out.shape[3]
    for k in range(cell_size):
        spot = slice(k * share, (k + 1) * share)
        part = [terms[:step, spot], terms[step:, spot]]
        if width > 2 * share:
            part.append(jnp.zeros((step, width - 2 * share), jnp.float32))
        part = jnp.concatenate(part, axis=1)
        for o in range(outers):
            term_out[k, o] = part[o : o + 1]
    term_slots[group] = term_out[cell_me, pl.ds(inner_me * kept, kept)]
    term_copies = [
        send(
            term_out.at[lax.rem(index, cell_size), pl.ds(lax.div(index, cell_size) * kept, kept)],
            term_slots.at[group], device, term_sems, d,
        )
        for d, (index, device) in enumerate(group_others)
    ]
    finish(kept_copies)
    for date in range(2):
        for q in range(kept):
            reserve[date, q] = jnp.sum(kept_slots[date, :, q], axis=0)
    finish(term_copies)
    for q in range(kept):
        mine = jnp.sum(term_slots[:, q], axis=0)
        for date in range(2):
            block[date, q] = mine[:, date * share : (date + 1) * share]
    finish(total_copies)
    across = jnp.sum(slots_two[...], axis=0)
    if not direct:
        loss_slots[outer_me] = across
        finish(
            [
                send(loss_slots.at[outer_me], loss_slots.at[outer_me], device, loss_sems, d)
                for d, (_, device) in enumerate(outer_others)
            ]
        )
        across = jnp.sum(loss_slots[...], axis=0)
    count = outers * outer_size
    lane = lax.broadcasted_iota(jnp.int32, (count, LANES), 1)
    row = lax.broadcasted_iota(jnp.int32, (count, LANES), 0)
    losses = jnp.sum(jnp.where(lane == row, across, 0.0), axis=1, keepdims=True)
    ahead = ((across > losses) | ((across == losses) & (lane < row))) & (lane < count)
    rank = jnp.sum(jnp.where(ahead, 1.0, 0.0), axis=1, keepdims=True)
    top = count // 4
    taken = jnp.sum(jnp.where(rank < top, losses, 0.0), axis=0, keepdims=True) / top
    capital[...] = jnp.broadcast_to(taken, capital.shape)


def settle(reserve, block, capital, reserve_out, block_out, capital_out, single, sems):
    single[...] = capital[:, :1]
    copies = [
        pltpu.make_async_copy(source, target, sems.at[i])
        for i, (source, target) in enumerate(
            [(reserve, reserve_out), (block, block_out), (single, capital_out)]
        )
    ]
    for copy in copies:
        copy.start()
    finish(copies)


def body(
    premium, charge, mortality, lapse_table, lapse_index, guarantee_type, block_index,
    account_start, guarantee_start, fee_rate, first_rates, second_rates, world_rates, spread,
):
    months_local, cells_local = premium.shape
    outer_size, inner_size, cell_size = (lax.axis_size(axis) for axis in ("outer", "inner", "cell"))
    months = months_local * outer_size
    group_size = inner_size * cell_size
    outers, paths = first_rates.shape[:2]
    paths_all = paths * inner_size
    cells_all = cells_local * cell_size
    width = 4 * LANES
    kept = outers // inner_size
    blocks = 4 * cells_all // BLOCK
    share = blocks // cell_size
    wide = -(-2 * share // LANES) * LANES
    everyone = outer_size * group_size
    wide_count = everyone if everyone <= DIRECT else group_size
    f32, i32 = jnp.float32, jnp.int32
    shape = jax.ShapeDtypeStruct

    def row(x):
        return x.reshape(1, -1)

    def buffer(*dims, dtype=f32):
        return pltpu.VMEM(dims, dtype)

    def sems(count):
        return pltpu.SemaphoreType.DMA((2, max(count, 1)))

    chunks = cells_local // width
    plan_count = 2 * chunks * (outer_size - 1)
    plan = buffer(months, cells_local)
    gathered = buffer(outer_size, months_local, cells_local)
    line, code = buffer(1, cells_local), buffer(1, cells_local, dtype=i32)
    total_rows = outers * paths
    first_months, second_months = first_rates.shape[2], second_rates.shape[2]
    operands = (
        premium, charge, mortality, lapse_table, row(lapse_index), row(guarantee_type), row(block_index),
        row(account_start), row(guarantee_start), row(fee_rate),
        first_rates.reshape(total_rows, -1), second_rates.reshape(total_rows, -1), world_rates, row(spread),
    )
    reserve, block, capital = pl.pallas_call(
        functools.partial(whole_kernel, outers, paths, paths_all, cells_all, width),
        out_shape=[
            shape((2, kept, 1, cells_local), f32), shape((2, kept, 1, share), f32), shape((1, LANES), f32),
        ],
        in_specs=[pl.BlockSpec(memory_space=pl.ANY)] * len(operands),
        out_specs=[VMEM] * 3,
        scratch_shapes=[
            buffer(months_local, cells_local), buffer(months_local, cells_local), buffer(*lapse_table.shape),
            code, code, code, line, line, line,
            buffer(total_rows, first_months), buffer(total_rows, second_months),
            buffer(*world_rates.shape), buffer(1, outers),
            gathered, gathered, plan, plan, plan, plan, buffer(ROWS, cells_local),
            buffer(3, ROWS, cells_local), buffer(3, ROWS, cells_local),
            buffer(first_months, total_rows, LANES), buffer(first_months, total_rows, LANES),
            buffer(second_months, total_rows, LANES), buffer(second_months, total_rows, LANES),
            buffer(PERIOD + 2 * ROWS, width), buffer(PERIOD, ROWS, LANES),
            buffer(outers, ROWS, cells_local), buffer(outers, 1, cells_local), buffer(outers, 1, cells_local),
            buffer(2, group_size, ROWS, LANES), buffer(wide_count, 1, LANES),
            buffer(2, inner_size, kept, 1, cells_local), buffer(blocks, cells_local, dtype=jnp.bfloat16),
            buffer(group_size, kept, 1, wide), buffer(cell_size, outers, 1, wide),
            buffer(outer_size, 1, LANES),
            pltpu.SemaphoreType.DMA((len(operands),)), sems(plan_count), sems(plan_count),
            sems(2 * (group_size - 1)), sems(wide_count - 1), sems(2 * (inner_size - 1)),
            sems(group_size - 1), sems(outer_size - 1), pltpu.SemaphoreType.REGULAR((max(cell_size - 1, 1),)),
        ],
        compiler_params=pltpu.CompilerParams(
            collective_id=0, has_side_effects=True, vmem_limit_bytes=24*2**20
        ),
    )(*[pltpu.with_memory_space_constraint(x, pltpu.HBM) for x in operands])
    reserve, block, capital = pl.pallas_call(
        settle,
        out_shape=[shape(reserve.shape, f32), shape(block.shape, f32), shape((1, 1), f32)],
        in_specs=[VMEM] * 3,
        out_specs=[pl.BlockSpec(memory_space=pltpu.HBM)] * 3,
        scratch_shapes=[buffer(1, 1), pltpu.SemaphoreType.DMA((3,))],
        compiler_params=pltpu.CompilerParams(vmem_limit_bytes=2**20),
    )(reserve, block, capital)
    return (
        reserve.reshape(2, kept, cells_local),
        block.reshape(2, kept, share),
        capital.reshape(1),
    )


def solution(mesh):
    placed = (
        P("outer", "cell"), P("outer", "cell"), P("outer", "cell"), P(), P("cell"), P("cell"), P("cell"),
        P("cell"), P("cell"), P("cell"), P("outer", "inner", None), P("outer", "inner", None),
        P("outer", None), P("outer"),
    )
    return jax.shard_map(
        body,
        mesh=mesh,
        in_specs=placed,
        out_specs=(P(None, ("outer", "inner"), "cell"), P(None, ("outer", "inner"), "cell"), P()),
        check_vma=False,
    )
```

```python
import functools
import jax
import jax.numpy as jnp
from jax import lax
from jax.experimental import pallas as pl
from jax.experimental.pallas import tpu as pltpu
from jax.sharding import PartitionSpec as P

PERIOD = 12
BLOCK = 128
LANES = 128
ROWS = 8
DIRECT = 32

credit_floor = 0.001
rollup_growth = 0.05
VMEM = pl.BlockSpec(memory_space=pltpu.VMEM)


def tiles(x, count):
    return jnp.concatenate([x] * count, axis=1)


def month(account, surviving, growth, nf, om, lb, keep, inverse):
    credited = jnp.maximum(account * keep + nf, 0.0) * growth
    lapse = lb * jnp.clip(credited * inverse, 0.5, 1.5)
    return credited, surviving * (om - lapse)


def claims_of(account, credited, surviving, guarantee, mf):
    return surviving * (mf * jnp.maximum(guarantee - credited, 0.0) - account)


def anniversary(account, guarantee, ratchet, rollup):
    return (
        guarantee
        + ratchet * (jnp.maximum(guarantee, account) - guarantee)
        + rollup * rollup_growth * guarantee
    )


def prefix(rates):
    months = rates.shape[1]
    tri = (
        lax.broadcasted_iota(jnp.int32, (months, months), 0)
        <= lax.broadcasted_iota(jnp.int32, (months, months), 1)
    ).astype(jnp.float32)
    return jnp.dot(rates, tri, precision=lax.Precision.HIGHEST, preferred_element_type=jnp.float32)


def spread_lanes(values, target, rows):
    for m in range(values.shape[1]):
        target[m, rows, :] = jnp.broadcast_to(values[:, m : m + 1], (values.shape[0], LANES))


def year(start, plans, cell, growth_lanes, first_month, state, width, begin, end):
    nf_ref, mf_ref, om_ref, lb_ref = plans
    repeat = width // LANES

    def chunk(j, _):
        cols = pl.ds(pl.multiple_of(j * width, width), width)
        account, surviving, guarantee = start(cols)
        keep, ratchet, rollup = cell[0:1, cols], cell[1:2, cols], cell[2:3, cols]
        inverse = 1.0 / guarantee
        for m in range(PERIOD):
            row = slice(first_month + m, first_month + m + 1)
            account, surviving = month(
                account,
                surviving,
                tiles(growth_lanes[m], repeat),
                nf_ref[row, cols],
                om_ref[row, cols],
                lb_ref[row, cols],
                keep,
                inverse,
            )
        state[0, :, cols] = account
        state[1, :, cols] = surviving
        state[2, :, cols] = anniversary(account, guarantee, ratchet, rollup)
        return 0

    lax.fori_loop(begin, end, chunk, 0)


def inner(state, plans, cell, gb, db, first_month, low, high, paths, sums, width, begin, end, flows):
    nf_ref, mf_ref, om_ref, lb_ref = plans
    repeat = width // LANES
    months = db.shape[0]
    groups = paths // ROWS
    chunks = end - begin
    base = first_month // ROWS * ROWS
    top = -(-(first_month + PERIOD) // ROWS) * ROWS

    def block(step, _):
        o, j = low + step // chunks, begin + step % chunks
        cols = pl.ds(pl.multiple_of(j * width, width), width)
        keep, ratchet, rollup = cell[0:1, cols], cell[1:2, cols], cell[2:3, cols]
        shape = (ROWS, width)
        one = pl.ds(o, 1)
        guarantee = state[2, one, cols]
        across = 1.0 / guarantee
        flows[: top - base, :width] = nf_ref[base:top, cols] * across
        ratio = [jnp.broadcast_to(state[0, one, cols] * across, shape)] * groups
        weight = [jnp.broadcast_to(state[1, one, cols] * guarantee, shape)] * groups
        inverse = [jnp.broadcast_to(across, shape)] * groups
        rows = [pl.ds(pl.multiple_of(o * paths + g * ROWS, ROWS), ROWS) for g in range(groups)]
        present = jnp.zeros(shape, jnp.float32)
        for m in range(months):
            row = slice(first_month + m, first_month + m + 1)
            mf, om, lb = mf_ref[row, cols], om_ref[row, cols], lb_ref[row, cols]
            for g in range(groups):
                if m < PERIOD:
                    at = first_month - base + m
                    nf = flows[at : at + 1, :width]
                else:
                    nf = nf_ref[row, cols] * inverse[g]
                before, alive = ratio[g], weight[g]
                after = jnp.maximum(before * keep + nf, 0.0) * tiles(gb[m, rows[g], :], repeat)
                weight[g] = alive * (om - lb * jnp.clip(after, 0.5, 1.5))
                claims = alive * (mf * jnp.maximum(1.0 - after, 0.0) - before)
                present = present + tiles(db[m, rows[g], :], repeat) * claims
                ratio[g] = after
            if (m + 1) % PERIOD == 0 and m + 1 < months:
                for g in range(groups):
                    lift = 1.0 + ratchet * (jnp.maximum(ratio[g], 1.0) - 1.0) + rollup * rollup_growth
                    drop = 1.0 / lift
                    ratio[g] = ratio[g] * drop
                    weight[g] = weight[g] * lift
                    inverse[g] = inverse[g] * drop
        sums[o, :, cols] = present
        return 0

    lax.fori_loop(0, (high - low) * chunks, block, 0)


def reduce_rows(sums, out, low, high, scale):
    for o in range(low, high):
        out[o] = jnp.sum(sums[o], axis=0, keepdims=True) * scale


def fill_growth(rates_ref, spread_column, gb, low, high, paths):
    for o in range(low, high):
        for g in range(paths // ROWS):
            rows = slice(o * paths + g * ROWS, o * paths + (g + 1) * ROWS)
            spread_lanes(
                1.0 + jnp.maximum(rates_ref[rows, :] - spread_column[o : o + 1], credit_floor), gb, rows
            )


def fill_later_growth(rates_lanes, spread_column, gb, low, high, paths):
    for o in range(low, high):
        rows = slice(o * paths, (o + 1) * paths)
        less = jnp.broadcast_to(spread_column[o : o + 1], (paths, LANES))
        for m in range(rates_lanes.shape[0]):
            gb[m, rows, :] = 1.0 + jnp.maximum(rates_lanes[m, rows, :] - less, credit_floor)


def fill_discount(rates_ref, db):
    discount = jnp.exp(-prefix(rates_ref[...]))
    for at in range(0, discount.shape[0], ROWS):
        spread_lanes(discount[at : at + ROWS], db, slice(at, at + ROWS))


def spans_of(total, width):
    head = width // 2
    spans = [(0, head), (head, head)] if head % (2 * LANES) == 0 else [(0, width)]
    return spans + [(begin, width) for begin in range(width, total, width)]


def peers(axes):
    sizes = [lax.axis_size(axis) for axis in axes]
    count = 1
    place = 0
    for axis, size in zip(axes, sizes):
        place = place * size + lax.axis_index(axis)
        count *= size
    others = []
    for distance in range(1, count):
        index = lax.rem(place + distance, count)
        rest, device = index, {}
        for axis, size in reversed(list(zip(axes, sizes))):
            device[axis] = lax.rem(rest, size)
            rest = lax.div(rest, size)
        others.append((index, device))
    return place, others


def greet(groups):
    barrier = pltpu.get_barrier_semaphore()
    count = 0
    for others in groups:
        for _, device in others:
            pl.semaphore_signal(barrier, inc=1, device_id=device, device_id_type=pl.DeviceIdType.MESH)
            count += 1
    return barrier, count


def beside(me, size, act):
    @pl.when(me > 0)
    def _():
        act({"cell": me - 1})

    @pl.when(me < size - 1)
    def _():
        act({"cell": me + 1})

    return (me > 0).astype(jnp.int32) + (me < size - 1).astype(jnp.int32)


def signal_to(sem):
    def act(device):
        pl.semaphore_signal(sem, inc=1, device_id=device, device_id_type=pl.DeviceIdType.MESH)

    return act


def send(source, target, device, sems, at):
    copy = pltpu.make_async_remote_copy(
        src_ref=source,
        dst_ref=target,
        send_sem=sems.at[0, at],
        recv_sem=sems.at[1, at],
        device_id=device,
        device_id_type=pl.DeviceIdType.MESH,
    )
    copy.start()
    return copy


def finish(copies):
    for copy in copies:
        copy.wait()


def local_totals(partial, low, high):
    zero = jnp.zeros((1, LANES), jnp.float32)
    rows = [
        jnp.broadcast_to(jnp.sum(partial[o], axis=1, keepdims=True), (1, LANES)) if low <= o < high else zero
        for o in range(ROWS)
    ]
    return jnp.concatenate(rows, axis=0)


def whole_kernel(
    outers, paths, paths_all, cells_all, width,
    premium, charge, mortality, table_in, lapse_in, type_in, block_in, account_in, guarantee_in, fee_in,
    first_in, second_in, world_in, spread_in,
    reserve, block, capital,
    v_premium, v_charge, table, lapse, kind, block_row, account, guarantee, fee,
    first_rates, second_rates, world, spread,
    nf_all, mort_all, nf_ref, mf_ref, om_ref, lb_ref, cell, state_one, state_two,
    gb, db_one, db_two, rb_two, flows, gw, world_lanes, spread_wide, sums, first, second,
    slots_one, slots_two, kept_slots, hot, term_slots, term_out, loss_slots,
    load_sems, plan_sems, pass_sems, one_sems, total_sems, kept_sems, term_sems, loss_sems, relay_sems,
):
    outer_size, months_local, cells_local = nf_all.shape
    inner_size = kept_slots.shape[1]
    cell_size = term_out.shape[0]
    kept = reserve.shape[1]
    blocks = hot.shape[0]
    share = block.shape[3]
    group, group_others = peers(("inner", "cell"))
    inner_me, inner_others = peers(("inner",))
    cell_me, cell_others = peers(("cell",))
    outer_me, outer_others = peers(("outer",))
    direct = slots_two.shape[0] > inner_size * cell_size
    all_me, all_others = peers(("outer", "inner", "cell")) if direct else (group, group_others)
    barrier, arrivals = greet([inner_others, outer_others])
    arrivals = arrivals + beside(cell_me, cell_size, signal_to(barrier))
    loads = [
        pltpu.make_async_copy(source, target, load_sems.at[i])
        for i, (source, target) in enumerate(
            [
                (premium, v_premium), (charge, v_charge), (mortality, mort_all.at[outer_me]),
                (table_in, table), (lapse_in, lapse), (type_in, kind), (block_in, block_row),
                (account_in, account), (guarantee_in, guarantee), (fee_in, fee),
                (first_in, first_rates), (second_in, second_rates), (world_in, world), (spread_in, spread),
            ]
        )
    ]
    for copy in loads:
        copy.start()
    finish(loads[:3])
    nf_all[outer_me] = v_premium[...] - v_charge[...]
    pl.semaphore_wait(barrier, arrivals)

    pair = inner_size % 2 == 0
    chunks = cells_local // width
    spans = spans_of(cells_local, width)
    side = lax.rem(inner_me, 2) if pair else 0
    plan_copies = []
    for j, (begin, size) in enumerate(spans):
        part = size // 2 if pair else size
        mine = pl.ds(pl.multiple_of(begin + side * part, part), part)
        copies = []
        for d, (_, device) in enumerate(outer_others):
            for k, plan in enumerate((nf_all, mort_all)):
                piece = plan.at[outer_me, :, mine]
                slot = (j * len(outer_others) + d) * 2 + k
                copies.append((d, plan, mine, slot, send(piece, piece, device, plan_sems, slot)))
        plan_copies.append(copies)
    pass_copies = []

    def pass_on(j):
        copies = []
        for d, plan, mine, slot, copy in plan_copies[j]:
            copy.wait_recv()
            if pair:
                source = lax.rem(outer_me + outer_size - 1 - d, outer_size)
                piece = plan.at[source, :, mine]
                partner = {"inner": inner_me + 1 - 2 * side}
                copies.append(send(piece, piece, partner, pass_sems, slot))
        pass_copies.append(copies)

    rounds = relay_sems.shape[0]

    def relay(low, high):
        for r in range(low, min(high, rounds)):
            pl.semaphore_wait(relay_sems.at[r - 1], near)
            beside(cell_me, cell_size, signal_to(relay_sems.at[r]))

    near = beside(cell_me, cell_size, signal_to(relay_sems.at[0]))
    finish(loads[3:])
    fee_row = fee[...]
    cell[0:1, :] = 1.0 - fee_row
    cell[1:2, :] = (kind[...] == 1).astype(jnp.float32)
    cell[2:3, :] = (kind[...] == 2).astype(jnp.float32)
    lapse_hot = (
        lax.broadcasted_iota(jnp.int32, (table.shape[0], cells_local), 0) == lapse[...]
    ).astype(jnp.float32)
    lb_ref[...] = lax.dot_general(
        table[...], lapse_hot, (((0,), (0,)), ((), ())),
        precision=lax.Precision.HIGHEST, preferred_element_type=jnp.float32,
    )
    world_rows = jnp.concatenate(
        [world[...], jnp.zeros((ROWS - outers, world.shape[1]), jnp.float32)], axis=0
    )
    diagonal = lax.broadcasted_iota(jnp.int32, (ROWS, outers), 0) == lax.broadcasted_iota(
        jnp.int32, (ROWS, outers), 1
    )
    spread_one = jnp.sum(jnp.where(diagonal, spread[...], 0.0), axis=1, keepdims=True)
    everything = slice(0, ROWS)
    spread_lanes(1.0 + jnp.maximum(world_rows[:, :PERIOD] - spread_one, credit_floor), gw, everything)
    spread_lanes(world_rows[:, PERIOD : 2 * PERIOD], world_lanes, everything)
    spread_wide[...] = jnp.broadcast_to(spread_one, spread_wide.shape)
    fill_growth(first_rates, spread_one, gb, 0, outers, paths)
    fill_discount(first_rates, db_one)
    fill_discount(second_rates, db_two)
    for at in range(0, second_rates.shape[0], ROWS):
        spread_lanes(second_rates[at : at + ROWS, :], rb_two, slice(at, at + ROWS))
    hot[...] = (
        lax.broadcasted_iota(jnp.int32, (blocks, cells_local), 0) == block_row[...]
    ).astype(jnp.float32).astype(jnp.bfloat16)
    ahead = min(2, len(spans))
    for j in range(ahead):
        pass_on(j)
    relay(1, 2)
    death = 1.0 / fee_row
    plans = (nf_ref, mf_ref, om_ref, lb_ref)

    def prepare(j):
        for copy in pass_copies[j]:
            copy.wait_recv()
        begin, size = spans[j]
        cols = slice(begin, begin + size)
        for s in range(outer_size):
            rows = slice(s * months_local, (s + 1) * months_local)
            nf_ref[rows, cols] = nf_all[s, :, cols] * fee_row[:, cols]
            mf_ref[rows, cols] = mort_all[s, :, cols] * death[:, cols]
            om_ref[rows, cols] = 1.0 - mort_all[s, :, cols]

    def start_one(cols):
        scale = fee[0:1, cols]
        shape = (ROWS, cols.size)
        return (
            jnp.broadcast_to(account[0:1, cols] * scale, shape),
            jnp.ones(shape, jnp.float32),
            jnp.broadcast_to(guarantee[0:1, cols] * scale, shape),
        )

    def start_two(cols):
        return state_one[0, :, cols], state_one[1, :, cols], state_one[2, :, cols]

    split = -(-outers // 2)
    halves = [(low, high) for low, high in ((0, split), (split, outers)) if low < high]
    distances = len(group_others)
    one_copies = []
    for h, (low, high) in enumerate(halves):
        if h == 0:
            for j, (begin, size) in enumerate(spans):
                prepare(j)
                at = begin // size
                year(start_one, plans, cell, gw, 0, state_one, size, at, at + 1)
                inner(
                    state_one, plans, cell, gb, db_one, PERIOD, low, high, paths, sums, size, at, at + 1, flows
                )
                if j + ahead < len(spans):
                    pass_on(j + ahead)
                if j == 0:
                    relay(2, rounds)
        else:
            inner(state_one, plans, cell, gb, db_one, PERIOD, low, high, paths, sums, width, 0, chunks, flows)
        reduce_rows(sums, first, low, high, 1.0 / paths_all)
        slots_one[h, group] = local_totals(first, low, high)
        if h == 0:
            for copies in plan_copies:
                for piece in copies:
                    piece[4].wait_send()
            for copies in pass_copies:
                for copy in copies:
                    copy.wait_send()
            pl.semaphore_wait(relay_sems.at[rounds - 1], near)
        slot = slots_one.at[h, group]
        one_copies.append(
            [
                send(slot, slot, device, one_sems, h * distances + d)
                for d, (_, device) in enumerate(group_others)
            ]
        )
    kept_copies = []

    def send_kept(date, partial):
        for index, device in inner_others:
            kept_copies.append(
                send(
                    partial.at[pl.ds(index * kept, kept)], kept_slots.at[date, inner_me],
                    device, kept_sems, len(kept_copies),
                )
            )
        kept_slots[date, inner_me] = partial[pl.ds(inner_me * kept, kept)]

    send_kept(0, first)
    total_one = jnp.zeros((ROWS, LANES), jnp.float32)
    for h, (low, high) in enumerate(halves):
        finish(one_copies[h])
        total_one = total_one + jnp.sum(slots_one[h], axis=0)
        spread_two = spread_wide[...] * (1.0 + jnp.tanh(total_one / cells_all))
        for m in range(PERIOD):
            gw[m] = 1.0 + jnp.maximum(world_lanes[m] - spread_two, credit_floor)
        year(start_two, plans, cell, gw, PERIOD, state_two, width, 0, chunks)
        fill_later_growth(rb_two, spread_two, gb, low, high, paths)
        inner(state_two, plans, cell, gb, db_two, 2 * PERIOD, low, high, paths, sums, width, 0, chunks, flows)
        reduce_rows(sums, second, low, high, 1.0 / paths_all)
    discount = jnp.exp(-jnp.sum(world_rows[:, PERIOD:], axis=1, keepdims=True))
    mine_one = slots_one[0, group]
    for h in range(1, len(halves)):
        mine_one = mine_one + slots_one[h, group]
    mine_loss = (discount * local_totals(second, 0, outers) - mine_one) / cells_all
    own = lax.broadcasted_iota(jnp.int32, (ROWS, LANES), 0)
    own_lane = lax.broadcasted_iota(jnp.int32, (ROWS, LANES), 1) - outer_me * outers
    mine_loss = jnp.where((own == own_lane) & (own < outers), mine_loss, 0.0)
    place, others = (all_me, all_others) if direct else (group, group_others)
    slots_two[place] = jnp.sum(mine_loss, axis=0, keepdims=True)
    total_copies = [
        send(slots_two.at[place], slots_two.at[place], device, total_sems, d)
        for d, (_, device) in enumerate(others)
    ]
    send_kept(1, second)
    step = -(-outers // ROWS) * ROWS
    lines = 2 * step
    line = lax.broadcasted_iota(jnp.int32, (step, cells_local), 0)
    values = []
    for partial in (first, second):
        value = jnp.zeros((step, cells_local), jnp.float32)
        for o in range(outers):
            value = jnp.where(line == o, jnp.broadcast_to(partial[o], value.shape), value)
        values.append(value)
    value = jnp.concatenate(values, axis=0)
    high = value.astype(jnp.bfloat16).astype(jnp.float32)
    value = value - high
    middle = value.astype(jnp.bfloat16).astype(jnp.float32)
    stacked = jnp.concatenate([high, middle, value - middle], axis=0)
    products = lax.dot_general(
        stacked.astype(jnp.bfloat16), hot[...], (((1,), (1,)), ((), ())),
        preferred_element_type=jnp.float32,
    )
    terms = products[:lines] + products[lines : 2 * lines] + products[2 * lines :]
    width = term_out.shape[3]
    for k in range(cell_size):
        spot = slice(k * share, (k + 1) * share)
        part = [terms[:step, spot], terms[step:, spot]]
        if width > 2 * share:
            part.append(jnp.zeros((step, width - 2 * share), jnp.float32))
        part = jnp.concatenate(part, axis=1)
        for o in range(outers):
            term_out[k, o] = part[o : o + 1]
    term_slots[group] = term_out[cell_me, pl.ds(inner_me * kept, kept)]
    term_copies = [
        send(
            term_out.at[lax.rem(index, cell_size), pl.ds(lax.div(index, cell_size) * kept, kept)],
            term_slots.at[group], device, term_sems, d,
        )
        for d, (index, device) in enumerate(group_others)
    ]
    finish(kept_copies)
    for date in range(2):
        for q in range(kept):
            reserve[date, q] = jnp.sum(kept_slots[date, :, q], axis=0)
    finish(term_copies)
    for q in range(kept):
        mine = jnp.sum(term_slots[:, q], axis=0)
        for date in range(2):
            block[date, q] = mine[:, date * share : (date + 1) * share]
    finish(total_copies)
    across = jnp.sum(slots_two[...], axis=0)
    if not direct:
        loss_slots[outer_me] = across
        finish(
            [
                send(loss_slots.at[outer_me], loss_slots.at[outer_me], device, loss_sems, d)
                for d, (_, device) in enumerate(outer_others)
            ]
        )
        across = jnp.sum(loss_slots[...], axis=0)
    count = outers * outer_size
    lane = lax.broadcasted_iota(jnp.int32, (count, LANES), 1)
    row = lax.broadcasted_iota(jnp.int32, (count, LANES), 0)
    losses = jnp.sum(jnp.where(lane == row, across, 0.0), axis=1, keepdims=True)
    ahead = ((across > losses) | ((across == losses) & (lane < row))) & (lane < count)
    rank = jnp.sum(jnp.where(ahead, 1.0, 0.0), axis=1, keepdims=True)
    top = count // 4
    taken = jnp.sum(jnp.where(rank < top, losses, 0.0), axis=0, keepdims=True) / top
    capital[...] = jnp.broadcast_to(taken, capital.shape)


def settle(reserve, block, capital, reserve_out, block_out, capital_out, single, sems):
    single[...] = capital[:, :1]
    copies = [
        pltpu.make_async_copy(source, target, sems.at[i])
        for i, (source, target) in enumerate(
            [(reserve, reserve_out), (block, block_out), (single, capital_out)]
        )
    ]
    for copy in copies:
        copy.start()
    finish(copies)


def body(
    premium, charge, mortality, lapse_table, lapse_index, guarantee_type, block_index,
    account_start, guarantee_start, fee_rate, first_rates, second_rates, world_rates, spread,
):
    months_local, cells_local = premium.shape
    outer_size, inner_size, cell_size = (lax.axis_size(axis) for axis in ("outer", "inner", "cell"))
    months = months_local * outer_size
    group_size = inner_size * cell_size
    outers, paths = first_rates.shape[:2]
    paths_all = paths * inner_size
    cells_all = cells_local * cell_size
    width = 4 * LANES
    kept = outers // inner_size
    blocks = 4 * cells_all // BLOCK
    share = blocks // cell_size
    wide = -(-2 * share // LANES) * LANES
    everyone = outer_size * group_size
    wide_count = everyone if everyone <= DIRECT else group_size
    f32, i32 = jnp.float32, jnp.int32
    shape = jax.ShapeDtypeStruct

    def row(x):
        return x.reshape(1, -1)

    def buffer(*dims, dtype=f32):
        return pltpu.VMEM(dims, dtype)

    def sems(count):
        return pltpu.SemaphoreType.DMA((2, max(count, 1)))

    chunks = len(spans_of(cells_local, width))
    plan_count = 2 * chunks * (outer_size - 1)
    plan = buffer(months, cells_local)
    gathered = buffer(outer_size, months_local, cells_local)
    line, code = buffer(1, cells_local), buffer(1, cells_local, dtype=i32)
    total_rows = outers * paths
    first_months, second_months = first_rates.shape[2], second_rates.shape[2]
    operands = (
        premium, charge, mortality, lapse_table, row(lapse_index), row(guarantee_type), row(block_index),
        row(account_start), row(guarantee_start), row(fee_rate),
        first_rates.reshape(total_rows, -1), second_rates.reshape(total_rows, -1), world_rates, row(spread),
    )
    reserve, block, capital = pl.pallas_call(
        functools.partial(whole_kernel, outers, paths, paths_all, cells_all, width),
        out_shape=[
            shape((2, kept, 1, cells_local), f32), shape((2, kept, 1, share), f32), shape((1, LANES), f32),
        ],
        in_specs=[pl.BlockSpec(memory_space=pl.ANY)] * len(operands),
        out_specs=[VMEM] * 3,
        scratch_shapes=[
            buffer(months_local, cells_local), buffer(months_local, cells_local), buffer(*lapse_table.shape),
            code, code, code, line, line, line,
            buffer(total_rows, first_months), buffer(total_rows, second_months),
            buffer(*world_rates.shape), buffer(1, outers),
            gathered, gathered, plan, plan, plan, plan, buffer(ROWS, cells_local),
            buffer(3, ROWS, cells_local), buffer(3, ROWS, cells_local),
            buffer(first_months, total_rows, LANES), buffer(first_months, total_rows, LANES),
            buffer(second_months, total_rows, LANES), buffer(second_months, total_rows, LANES),
            buffer(PERIOD + 2 * ROWS, width), buffer(PERIOD, ROWS, LANES),
            buffer(PERIOD, ROWS, LANES), buffer(ROWS, LANES),
            buffer(outers, ROWS, cells_local), buffer(outers, 1, cells_local), buffer(outers, 1, cells_local),
            buffer(2, group_size, ROWS, LANES), buffer(wide_count, 1, LANES),
            buffer(2, inner_size, kept, 1, cells_local), buffer(blocks, cells_local, dtype=jnp.bfloat16),
            buffer(group_size, kept, 1, wide), buffer(cell_size, outers, 1, wide),
            buffer(outer_size, 1, LANES),
            pltpu.SemaphoreType.DMA((len(operands),)), sems(plan_count), sems(plan_count),
            sems(2 * (group_size - 1)), sems(wide_count - 1), sems(2 * (inner_size - 1)),
            sems(group_size - 1), sems(outer_size - 1), pltpu.SemaphoreType.REGULAR((max(cell_size - 1, 1),)),
        ],
        compiler_params=pltpu.CompilerParams(
            collective_id=0, has_side_effects=True, vmem_limit_bytes=24*2**20
        ),
    )(*[pltpu.with_memory_space_constraint(x, pltpu.HBM) for x in operands])
    reserve, block, capital = pl.pallas_call(
        settle,
        out_shape=[shape(reserve.shape, f32), shape(block.shape, f32), shape((1, 1), f32)],
        in_specs=[VMEM] * 3,
        out_specs=[pl.BlockSpec(memory_space=pltpu.HBM)] * 3,
        scratch_shapes=[buffer(1, 1), pltpu.SemaphoreType.DMA((3,))],
        compiler_params=pltpu.CompilerParams(vmem_limit_bytes=2**20),
    )(reserve, block, capital)
    return (
        reserve.reshape(2, kept, cells_local),
        block.reshape(2, kept, share),
        capital.reshape(1),
    )


def solution(mesh):
    placed = (
        P("outer", "cell"), P("outer", "cell"), P("outer", "cell"), P(), P("cell"), P("cell"), P("cell"),
        P("cell"), P("cell"), P("cell"), P("outer", "inner", None), P("outer", "inner", None),
        P("outer", None), P("outer"),
    )
    return jax.shard_map(
        body,
        mesh=mesh,
        in_specs=placed,
        out_specs=(P(None, ("outer", "inner"), "cell"), P(None, ("outer", "inner"), "cell"), P()),
        check_vma=False,
    )
```

```python
import functools
import jax
import jax.numpy as jnp
from jax import lax
from jax.experimental import pallas as pl
from jax.experimental.pallas import tpu as pltpu
from jax.sharding import PartitionSpec as P

PERIOD = 12
BLOCK = 128
LANES = 128
ROWS = 8
DIRECT = 32

credit_floor = 0.001
rollup_growth = 0.05
VMEM = pl.BlockSpec(memory_space=pltpu.VMEM)


def tiles(x, count):
    return jnp.concatenate([x] * count, axis=1)


def month(account, surviving, growth, nf, om, lb, keep, inverse):
    credited = jnp.maximum(account * keep + nf, 0.0) * growth
    lapse = lb * jnp.clip(credited * inverse, 0.5, 1.5)
    return credited, surviving * (om - lapse)


def claims_of(account, credited, surviving, guarantee, mf):
    return surviving * (mf * jnp.maximum(guarantee - credited, 0.0) - account)


def anniversary(account, guarantee, ratchet, rollup):
    return (
        guarantee
        + ratchet * (jnp.maximum(guarantee, account) - guarantee)
        + rollup * rollup_growth * guarantee
    )


def prefix(rates):
    months = rates.shape[1]
    tri = (
        lax.broadcasted_iota(jnp.int32, (months, months), 0)
        <= lax.broadcasted_iota(jnp.int32, (months, months), 1)
    ).astype(jnp.float32)
    return jnp.dot(rates, tri, precision=lax.Precision.HIGHEST, preferred_element_type=jnp.float32)


def spread_lanes(values, target, rows):
    for m in range(values.shape[1]):
        target[m, rows, :] = jnp.broadcast_to(values[:, m : m + 1], (values.shape[0], LANES))


def year(start, plans, cell, growth_lanes, first_month, state, width, begin, end):
    nf_ref, mf_ref, om_ref, lb_ref = plans
    repeat = width // LANES

    def chunk(j, _):
        cols = pl.ds(pl.multiple_of(j * width, width), width)
        account, surviving, guarantee = start(cols)
        keep, ratchet, rollup = cell[0:1, cols], cell[1:2, cols], cell[2:3, cols]
        inverse = 1.0 / guarantee
        for m in range(PERIOD):
            row = slice(first_month + m, first_month + m + 1)
            account, surviving = month(
                account,
                surviving,
                tiles(growth_lanes[m], repeat),
                nf_ref[row, cols],
                om_ref[row, cols],
                lb_ref[row, cols],
                keep,
                inverse,
            )
        state[0, :, cols] = account
        state[1, :, cols] = surviving
        state[2, :, cols] = anniversary(account, guarantee, ratchet, rollup)
        return 0

    lax.fori_loop(begin, end, chunk, 0)


def inner(state, plans, cell, gb, db, first_month, low, high, paths, sums, width, begin, end, flows):
    nf_ref, mf_ref, om_ref, lb_ref = plans
    repeat = width // LANES
    months = db.shape[0]
    groups = paths // ROWS
    chunks = end - begin
    base = first_month // ROWS * ROWS
    top = -(-(first_month + PERIOD) // ROWS) * ROWS

    def block(step, _):
        o, j = low + step // chunks, begin + step % chunks
        cols = pl.ds(pl.multiple_of(j * width, width), width)
        keep, ratchet, rollup = cell[0:1, cols], cell[1:2, cols], cell[2:3, cols]
        shape = (ROWS, width)
        one = pl.ds(o, 1)
        guarantee = state[2, one, cols]
        across = 1.0 / guarantee
        flows[: top - base, :width] = nf_ref[base:top, cols] * across
        ratio = [jnp.broadcast_to(state[0, one, cols] * across, shape)] * groups
        weight = [jnp.broadcast_to(state[1, one, cols] * guarantee, shape)] * groups
        inverse = [jnp.broadcast_to(across, shape)] * groups
        rows = [pl.ds(pl.multiple_of(o * paths + g * ROWS, ROWS), ROWS) for g in range(groups)]
        present = jnp.zeros(shape, jnp.float32)
        for m in range(months):
            row = slice(first_month + m, first_month + m + 1)
            mf, om, lb = mf_ref[row, cols], om_ref[row, cols], lb_ref[row, cols]
            for g in range(groups):
                if m < PERIOD:
                    at = first_month - base + m
                    nf = flows[at : at + 1, :width]
                else:
                    nf = nf_ref[row, cols] * inverse[g]
                before, alive = ratio[g], weight[g]
                after = jnp.maximum(before * keep + nf, 0.0) * tiles(gb[m, rows[g], :], repeat)
                weight[g] = alive * (om - lb * jnp.clip(after, 0.5, 1.5))
                claims = alive * (mf * jnp.maximum(1.0 - after, 0.0) - before)
                present = present + tiles(db[m, rows[g], :], repeat) * claims
                ratio[g] = after
            if (m + 1) % PERIOD == 0 and m + 1 < months:
                for g in range(groups):
                    lift = 1.0 + ratchet * (jnp.maximum(ratio[g], 1.0) - 1.0) + rollup * rollup_growth
                    drop = 1.0 / lift
                    ratio[g] = ratio[g] * drop
                    weight[g] = weight[g] * lift
                    inverse[g] = inverse[g] * drop
        sums[o, :, cols] = present
        return 0

    lax.fori_loop(0, (high - low) * chunks, block, 0)


def reduce_rows(sums, out, low, high, scale):
    for o in range(low, high):
        out[o] = jnp.sum(sums[o], axis=0, keepdims=True) * scale


def fill_growth(rates_ref, spread_column, gb, low, high, paths):
    for o in range(low, high):
        for g in range(paths // ROWS):
            rows = slice(o * paths + g * ROWS, o * paths + (g + 1) * ROWS)
            spread_lanes(
                1.0 + jnp.maximum(rates_ref[rows, :] - spread_column[o : o + 1], credit_floor), gb, rows
            )


def fill_later_growth(rates_lanes, spread_column, gb, low, high, paths):
    for o in range(low, high):
        rows = slice(o * paths, (o + 1) * paths)
        less = jnp.broadcast_to(spread_column[o : o + 1], (paths, LANES))
        for m in range(rates_lanes.shape[0]):
            gb[m, rows, :] = 1.0 + jnp.maximum(rates_lanes[m, rows, :] - less, credit_floor)


def fill_discount(rates_ref, db):
    discount = jnp.exp(-prefix(rates_ref[...]))
    for at in range(0, discount.shape[0], ROWS):
        spread_lanes(discount[at : at + ROWS], db, slice(at, at + ROWS))


def spans_of(total, width):
    head = width // 2
    spans = [(0, head), (head, head)] if head % (2 * LANES) == 0 else [(0, width)]
    return spans + [(begin, width) for begin in range(width, total, width)]


def peers(axes):
    sizes = [lax.axis_size(axis) for axis in axes]
    count = 1
    place = 0
    for axis, size in zip(axes, sizes):
        place = place * size + lax.axis_index(axis)
        count *= size
    others = []
    for distance in range(1, count):
        index = lax.rem(place + distance, count)
        rest, device = index, {}
        for axis, size in reversed(list(zip(axes, sizes))):
            device[axis] = lax.rem(rest, size)
            rest = lax.div(rest, size)
        others.append((index, device))
    return place, others


def greet(groups):
    barrier = pltpu.get_barrier_semaphore()
    count = 0
    for others in groups:
        for _, device in others:
            pl.semaphore_signal(barrier, inc=1, device_id=device, device_id_type=pl.DeviceIdType.MESH)
            count += 1
    return barrier, count


def beside(me, size, act):
    @pl.when(me > 0)
    def _():
        act({"cell": me - 1})

    @pl.when(me < size - 1)
    def _():
        act({"cell": me + 1})

    return (me > 0).astype(jnp.int32) + (me < size - 1).astype(jnp.int32)


def signal_to(sem):
    def act(device):
        pl.semaphore_signal(sem, inc=1, device_id=device, device_id_type=pl.DeviceIdType.MESH)

    return act


def send(source, target, device, sems, at):
    copy = pltpu.make_async_remote_copy(
        src_ref=source,
        dst_ref=target,
        send_sem=sems.at[0, at],
        recv_sem=sems.at[1, at],
        device_id=device,
        device_id_type=pl.DeviceIdType.MESH,
    )
    copy.start()
    return copy


def finish(copies):
    for copy in copies:
        copy.wait()


def local_totals(partial, low, high):
    zero = jnp.zeros((1, LANES), jnp.float32)
    rows = [
        jnp.broadcast_to(jnp.sum(partial[o], axis=1, keepdims=True), (1, LANES)) if low <= o < high else zero
        for o in range(ROWS)
    ]
    return jnp.concatenate(rows, axis=0)


def whole_kernel(
    outers, paths, paths_all, cells_all, width,
    premium, charge, mortality, table_in, lapse_in, type_in, block_in, account_in, guarantee_in, fee_in,
    first_in, second_in, world_in, spread_in,
    reserve, block, capital,
    v_premium, v_charge, table, lapse, kind, block_row, account, guarantee, fee,
    first_rates, second_rates, world, spread,
    nf_all, mort_all, nf_ref, mf_ref, om_ref, lb_ref, cell, state_one, state_two,
    gb, db_one, db_two, rb_two, flows, gw, world_lanes, spread_wide, sums, first, second,
    slots_one, slots_two, kept_slots, hot, term_slots, term_out, loss_slots,
    load_sems, plan_sems, pass_sems, one_sems, total_sems, kept_sems, term_sems, loss_sems, relay_sems,
):
    outer_size, months_local, cells_local = nf_all.shape
    inner_size = kept_slots.shape[1]
    cell_size = term_out.shape[0]
    kept = reserve.shape[1]
    blocks = hot.shape[0]
    share = block.shape[3]
    group, group_others = peers(("inner", "cell"))
    inner_me, inner_others = peers(("inner",))
    cell_me, cell_others = peers(("cell",))
    outer_me, outer_others = peers(("outer",))
    direct = slots_two.shape[0] > inner_size * cell_size
    all_me, all_others = peers(("outer", "inner", "cell")) if direct else (group, group_others)
    barrier, arrivals = greet([inner_others, outer_others])
    arrivals = arrivals + beside(cell_me, cell_size, signal_to(barrier))
    loads = [
        pltpu.make_async_copy(source, target, load_sems.at[i])
        for i, (source, target) in enumerate(
            [
                (premium, v_premium), (charge, v_charge), (mortality, mort_all.at[outer_me]),
                (table_in, table), (lapse_in, lapse), (type_in, kind), (block_in, block_row),
                (account_in, account), (guarantee_in, guarantee), (fee_in, fee),
                (first_in, first_rates), (second_in, second_rates), (world_in, world), (spread_in, spread),
            ]
        )
    ]
    for copy in loads:
        copy.start()
    finish(loads[:3])
    nf_all[outer_me] = v_premium[...] - v_charge[...]
    pl.semaphore_wait(barrier, arrivals)

    pair = inner_size % 2 == 0
    chunks = cells_local // width
    spans = spans_of(cells_local, width)
    side = lax.rem(inner_me, 2) if pair else 0
    plan_copies = []
    for j, (begin, size) in enumerate(spans):
        part = size // 2 if pair else size
        mine = pl.ds(pl.multiple_of(begin + side * part, part), part)
        copies = []
        for d, (_, device) in enumerate(outer_others):
            for k, plan in enumerate((nf_all, mort_all)):
                piece = plan.at[outer_me, :, mine]
                slot = (j * len(outer_others) + d) * 2 + k
                copies.append((d, plan, mine, slot, send(piece, piece, device, plan_sems, slot)))
        plan_copies.append(copies)
    pass_copies = []

    def pass_on(j):
        copies = []
        for d, plan, mine, slot, copy in plan_copies[j]:
            copy.wait_recv()
            if pair:
                source = lax.rem(outer_me + outer_size - 1 - d, outer_size)
                piece = plan.at[source, :, mine]
                partner = {"inner": inner_me + 1 - 2 * side}
                copies.append(send(piece, piece, partner, pass_sems, slot))
        pass_copies.append(copies)

    rounds = relay_sems.shape[0]

    def relay(low, high):
        for r in range(low, min(high, rounds)):
            pl.semaphore_wait(relay_sems.at[r - 1], near)
            beside(cell_me, cell_size, signal_to(relay_sems.at[r]))

    near = beside(cell_me, cell_size, signal_to(relay_sems.at[0]))
    finish(loads[3:])
    fee_row = fee[...]
    cell[0:1, :] = 1.0 - fee_row
    cell[1:2, :] = (kind[...] == 1).astype(jnp.float32)
    cell[2:3, :] = (kind[...] == 2).astype(jnp.float32)
    lapse_hot = (
        lax.broadcasted_iota(jnp.int32, (table.shape[0], cells_local), 0) == lapse[...]
    ).astype(jnp.float32)
    lb_ref[...] = lax.dot_general(
        table[...], lapse_hot, (((0,), (0,)), ((), ())),
        precision=lax.Precision.HIGHEST, preferred_element_type=jnp.float32,
    )
    world_rows = jnp.concatenate(
        [world[...], jnp.zeros((ROWS - outers, world.shape[1]), jnp.float32)], axis=0
    )
    diagonal = lax.broadcasted_iota(jnp.int32, (ROWS, outers), 0) == lax.broadcasted_iota(
        jnp.int32, (ROWS, outers), 1
    )
    spread_one = jnp.sum(jnp.where(diagonal, spread[...], 0.0), axis=1, keepdims=True)
    everything = slice(0, ROWS)
    spread_lanes(1.0 + jnp.maximum(world_rows[:, :PERIOD] - spread_one, credit_floor), gw, everything)
    spread_lanes(world_rows[:, PERIOD : 2 * PERIOD], world_lanes, everything)
    spread_wide[...] = jnp.broadcast_to(spread_one, spread_wide.shape)
    fill_growth(first_rates, spread_one, gb, 0, outers, paths)
    fill_discount(first_rates, db_one)
    fill_discount(second_rates, db_two)
    for at in range(0, second_rates.shape[0], ROWS):
        spread_lanes(second_rates[at : at + ROWS, :], rb_two, slice(at, at + ROWS))
    ahead = min(2, len(spans))
    for j in range(ahead):
        pass_on(j)
        if j == 0:
            hot[...] = (
                lax.broadcasted_iota(jnp.int32, (blocks, cells_local), 0) == block_row[...]
            ).astype(jnp.float32).astype(jnp.bfloat16)
    relay(1, 2)
    death = 1.0 / fee_row
    plans = (nf_ref, mf_ref, om_ref, lb_ref)

    def prepare(j):
        for copy in pass_copies[j]:
            copy.wait_recv()
        begin, size = spans[j]
        cols = slice(begin, begin + size)
        for s in range(outer_size):
            rows = slice(s * months_local, (s + 1) * months_local)
            nf_ref[rows, cols] = nf_all[s, :, cols] * fee_row[:, cols]
            mf_ref[rows, cols] = mort_all[s, :, cols] * death[:, cols]
            om_ref[rows, cols] = 1.0 - mort_all[s, :, cols]

    def start_one(cols):
        scale = fee[0:1, cols]
        shape = (ROWS, cols.size)
        return (
            jnp.broadcast_to(account[0:1, cols] * scale, shape),
            jnp.ones(shape, jnp.float32),
            jnp.broadcast_to(guarantee[0:1, cols] * scale, shape),
        )

    def start_two(cols):
        return state_one[0, :, cols], state_one[1, :, cols], state_one[2, :, cols]

    split = -(-outers // 2)
    halves = [(low, high) for low, high in ((0, split), (split, outers)) if low < high]
    distances = len(group_others)
    one_copies = []
    for h, (low, high) in enumerate(halves):
        if h == 0:
            for j, (begin, size) in enumerate(spans):
                prepare(j)
                at = begin // size
                year(start_one, plans, cell, gw, 0, state_one, size, at, at + 1)
                inner(
                    state_one, plans, cell, gb, db_one, PERIOD, low, high, paths, sums, size, at, at + 1, flows
                )
                if j + ahead < len(spans):
                    pass_on(j + ahead)
                if j == 0:
                    relay(2, rounds)
        else:
            inner(state_one, plans, cell, gb, db_one, PERIOD, low, high, paths, sums, width, 0, chunks, flows)
        reduce_rows(sums, first, low, high, 1.0 / paths_all)
        slots_one[h, group] = local_totals(first, low, high)
        if h == 0:
            for copies in plan_copies:
                for piece in copies:
                    piece[4].wait_send()
            for copies in pass_copies:
                for copy in copies:
                    copy.wait_send()
            pl.semaphore_wait(relay_sems.at[rounds - 1], near)
        slot = slots_one.at[h, group]
        one_copies.append(
            [
                send(slot, slot, device, one_sems, h * distances + d)
                for d, (_, device) in enumerate(group_others)
            ]
        )
    kept_copies = []

    def send_kept(date, partial):
        for index, device in inner_others:
            kept_copies.append(
                send(
                    partial.at[pl.ds(index * kept, kept)], kept_slots.at[date, inner_me],
                    device, kept_sems, len(kept_copies),
                )
            )
        kept_slots[date, inner_me] = partial[pl.ds(inner_me * kept, kept)]

    send_kept(0, first)
    total_one = jnp.zeros((ROWS, LANES), jnp.float32)
    for h, (low, high) in enumerate(halves):
        finish(one_copies[h])
        total_one = total_one + jnp.sum(slots_one[h], axis=0)
        spread_two = spread_wide[...] * (1.0 + jnp.tanh(total_one / cells_all))
        for m in range(PERIOD):
            gw[m] = 1.0 + jnp.maximum(world_lanes[m] - spread_two, credit_floor)
        year(start_two, plans, cell, gw, PERIOD, state_two, width, 0, chunks)
        fill_later_growth(rb_two, spread_two, gb, low, high, paths)
        inner(state_two, plans, cell, gb, db_two, 2 * PERIOD, low, high, paths, sums, width, 0, chunks, flows)
        reduce_rows(sums, second, low, high, 1.0 / paths_all)
    discount = jnp.exp(-jnp.sum(world_rows[:, PERIOD:], axis=1, keepdims=True))
    mine_one = slots_one[0, group]
    for h in range(1, len(halves)):
        mine_one = mine_one + slots_one[h, group]
    mine_loss = (discount * local_totals(second, 0, outers) - mine_one) / cells_all
    own = lax.broadcasted_iota(jnp.int32, (ROWS, LANES), 0)
    own_lane = lax.broadcasted_iota(jnp.int32, (ROWS, LANES), 1) - outer_me * outers
    mine_loss = jnp.where((own == own_lane) & (own < outers), mine_loss, 0.0)
    place, others = (all_me, all_others) if direct else (group, group_others)
    slots_two[place] = jnp.sum(mine_loss, axis=0, keepdims=True)
    total_copies = [
        send(slots_two.at[place], slots_two.at[place], device, total_sems, d)
        for d, (_, device) in enumerate(others[::-1])
    ]
    send_kept(1, second)
    step = -(-outers // ROWS) * ROWS
    lines = 2 * step
    line = lax.broadcasted_iota(jnp.int32, (step, cells_local), 0)
    values = []
    for partial in (first, second):
        value = jnp.zeros((step, cells_local), jnp.float32)
        for o in range(outers):
            value = jnp.where(line == o, jnp.broadcast_to(partial[o], value.shape), value)
        values.append(value)
    value = jnp.concatenate(values, axis=0)
    high = value.astype(jnp.bfloat16).astype(jnp.float32)
    value = value - high
    middle = value.astype(jnp.bfloat16).astype(jnp.float32)
    stacked = jnp.concatenate([high, middle, value - middle], axis=0)
    products = lax.dot_general(
        stacked.astype(jnp.bfloat16), hot[...], (((1,), (1,)), ((), ())),
        preferred_element_type=jnp.float32,
    )
    terms = products[:lines] + products[lines : 2 * lines] + products[2 * lines :]
    width = term_out.shape[3]
    for k in range(cell_size):
        spot = slice(k * share, (k + 1) * share)
        part = [terms[:step, spot], terms[step:, spot]]
        if width > 2 * share:
            part.append(jnp.zeros((step, width - 2 * share), jnp.float32))
        part = jnp.concatenate(part, axis=1)
        for o in range(outers):
            term_out[k, o] = part[o : o + 1]
    term_slots[group] = term_out[cell_me, pl.ds(inner_me * kept, kept)]
    term_copies = [
        send(
            term_out.at[lax.rem(index, cell_size), pl.ds(lax.div(index, cell_size) * kept, kept)],
            term_slots.at[group], device, term_sems, d,
        )
        for d, (index, device) in enumerate(group_others)
    ]
    finish(kept_copies)
    for date in range(2):
        for q in range(kept):
            reserve[date, q] = jnp.sum(kept_slots[date, :, q], axis=0)
    finish(term_copies)
    for q in range(kept):
        mine = jnp.sum(term_slots[:, q], axis=0)
        for date in range(2):
            block[date, q] = mine[:, date * share : (date + 1) * share]
    finish(total_copies)
    across = jnp.sum(slots_two[...], axis=0)
    if not direct:
        loss_slots[outer_me] = across
        finish(
            [
                send(loss_slots.at[outer_me], loss_slots.at[outer_me], device, loss_sems, d)
                for d, (_, device) in enumerate(outer_others)
            ]
        )
        across = jnp.sum(loss_slots[...], axis=0)
    count = outers * outer_size
    lane = lax.broadcasted_iota(jnp.int32, (count, LANES), 1)
    row = lax.broadcasted_iota(jnp.int32, (count, LANES), 0)
    losses = jnp.sum(jnp.where(lane == row, across, 0.0), axis=1, keepdims=True)
    ahead = ((across > losses) | ((across == losses) & (lane < row))) & (lane < count)
    rank = jnp.sum(jnp.where(ahead, 1.0, 0.0), axis=1, keepdims=True)
    top = count // 4
    taken = jnp.sum(jnp.where(rank < top, losses, 0.0), axis=0, keepdims=True) / top
    capital[...] = jnp.broadcast_to(taken, capital.shape)


def settle(reserve, block, capital, reserve_out, block_out, capital_out, single, sems):
    single[...] = capital[:, :1]
    copies = [
        pltpu.make_async_copy(source, target, sems.at[i])
        for i, (source, target) in enumerate(
            [(reserve, reserve_out), (block, block_out), (single, capital_out)]
        )
    ]
    for copy in copies:
        copy.start()
    finish(copies)


def body(
    premium, charge, mortality, lapse_table, lapse_index, guarantee_type, block_index,
    account_start, guarantee_start, fee_rate, first_rates, second_rates, world_rates, spread,
):
    months_local, cells_local = premium.shape
    outer_size, inner_size, cell_size = (lax.axis_size(axis) for axis in ("outer", "inner", "cell"))
    months = months_local * outer_size
    group_size = inner_size * cell_size
    outers, paths = first_rates.shape[:2]
    paths_all = paths * inner_size
    cells_all = cells_local * cell_size
    width = 4 * LANES
    kept = outers // inner_size
    blocks = 4 * cells_all // BLOCK
    share = blocks // cell_size
    wide = -(-2 * share // LANES) * LANES
    everyone = outer_size * group_size
    wide_count = everyone if everyone <= DIRECT else group_size
    f32, i32 = jnp.float32, jnp.int32
    shape = jax.ShapeDtypeStruct

    def row(x):
        return x.reshape(1, -1)

    def buffer(*dims, dtype=f32):
        return pltpu.VMEM(dims, dtype)

    def sems(count):
        return pltpu.SemaphoreType.DMA((2, max(count, 1)))

    chunks = len(spans_of(cells_local, width))
    plan_count = 2 * chunks * (outer_size - 1)
    plan = buffer(months, cells_local)
    gathered = buffer(outer_size, months_local, cells_local)
    line, code = buffer(1, cells_local), buffer(1, cells_local, dtype=i32)
    total_rows = outers * paths
    first_months, second_months = first_rates.shape[2], second_rates.shape[2]
    operands = (
        premium, charge, mortality, lapse_table, row(lapse_index), row(guarantee_type), row(block_index),
        row(account_start), row(guarantee_start), row(fee_rate),
        first_rates.reshape(total_rows, -1), second_rates.reshape(total_rows, -1), world_rates, row(spread),
    )
    reserve, block, capital = pl.pallas_call(
        functools.partial(whole_kernel, outers, paths, paths_all, cells_all, width),
        out_shape=[
            shape((2, kept, 1, cells_local), f32), shape((2, kept, 1, share), f32), shape((1, LANES), f32),
        ],
        in_specs=[pl.BlockSpec(memory_space=pl.ANY)] * len(operands),
        out_specs=[VMEM] * 3,
        scratch_shapes=[
            buffer(months_local, cells_local), buffer(months_local, cells_local), buffer(*lapse_table.shape),
            code, code, code, line, line, line,
            buffer(total_rows, first_months), buffer(total_rows, second_months),
            buffer(*world_rates.shape), buffer(1, outers),
            gathered, gathered, plan, plan, plan, plan, buffer(ROWS, cells_local),
            buffer(3, ROWS, cells_local), buffer(3, ROWS, cells_local),
            buffer(first_months, total_rows, LANES), buffer(first_months, total_rows, LANES),
            buffer(second_months, total_rows, LANES), buffer(second_months, total_rows, LANES),
            buffer(PERIOD + 2 * ROWS, width), buffer(PERIOD, ROWS, LANES),
            buffer(PERIOD, ROWS, LANES), buffer(ROWS, LANES),
            buffer(outers, ROWS, cells_local), buffer(outers, 1, cells_local), buffer(outers, 1, cells_local),
            buffer(2, group_size, ROWS, LANES), buffer(wide_count, 1, LANES),
            buffer(2, inner_size, kept, 1, cells_local), buffer(blocks, cells_local, dtype=jnp.bfloat16),
            buffer(group_size, kept, 1, wide), buffer(cell_size, outers, 1, wide),
            buffer(outer_size, 1, LANES),
            pltpu.SemaphoreType.DMA((len(operands),)), sems(plan_count), sems(plan_count),
            sems(2 * (group_size - 1)), sems(wide_count - 1), sems(2 * (inner_size - 1)),
            sems(group_size - 1), sems(outer_size - 1), pltpu.SemaphoreType.REGULAR((max(cell_size - 1, 1),)),
        ],
        compiler_params=pltpu.CompilerParams(
            collective_id=0, has_side_effects=True, vmem_limit_bytes=24*2**20
        ),
    )(*[pltpu.with_memory_space_constraint(x, pltpu.HBM) for x in operands])
    reserve, block, capital = pl.pallas_call(
        settle,
        out_shape=[shape(reserve.shape, f32), shape(block.shape, f32), shape((1, 1), f32)],
        in_specs=[VMEM] * 3,
        out_specs=[pl.BlockSpec(memory_space=pltpu.HBM)] * 3,
        scratch_shapes=[buffer(1, 1), pltpu.SemaphoreType.DMA((3,))],
        compiler_params=pltpu.CompilerParams(vmem_limit_bytes=2**20),
    )(reserve, block, capital)
    return (
        reserve.reshape(2, kept, cells_local),
        block.reshape(2, kept, share),
        capital.reshape(1),
    )


def solution(mesh):
    placed = (
        P("outer", "cell"), P("outer", "cell"), P("outer", "cell"), P(), P("cell"), P("cell"), P("cell"),
        P("cell"), P("cell"), P("cell"), P("outer", "inner", None), P("outer", "inner", None),
        P("outer", None), P("outer"),
    )
    return jax.shard_map(
        body,
        mesh=mesh,
        in_specs=placed,
        out_specs=(P(None, ("outer", "inner"), "cell"), P(None, ("outer", "inner"), "cell"), P()),
        check_vma=False,
    )
```
